32 devices in a mesh: sim: 2 (over y), grp: 4 (over z), gz: 4 (over x, core).
Axes of the slice: x: 2, y: 2, z: 4, core: 2. Of those that a mesh axis runs over, the one named last changes fastest.
Arguments:
- fields: float32 [8, 2, 1024, 1024], P(None, None, 'sim', ('grp', 'gz')), may hold values from -6 to 6
- diffusivity: float32 [8], replicated, may hold values from 0.03 to 0.12
- velocity: float32 [2, 8], replicated, may hold values from -0.4 to 0.4
- coupling: float32 [8, 8], replicated, may hold values from -0.6 to 0.6
- basis_x: bfloat16 [1024, 128], replicated, may hold values from -0.1875 to 0.1875
- basis_y: bfloat16 [1024, 128], replicated, may hold values from -0.1875 to 0.1875
Outputs:
- fields_out: float32 [8, 2, 1024, 1024], P(None, None, 'sim', ('grp', 'gz'))
- gram_x: float32 [1024, 1024], P('sim', ('grp', 'gz'))
- gram_y: float32 [1024, 1024], P(('grp', 'gz'), 'sim')
- core: float32 [8, 2, 128, 128], P(None, None, 'sim', ('grp', 'gz'))
The draws below stay inside these ranges and needn't reach their ends.
All inputs are finite; a program needn't handle non-finite values.
Results may differ from the reference program's by a relative error of at most 0.0003.
Values sent between devices are 32-bit elements; how exact they have to be, the bound alone decides.
No kernel may reach another device: no remote copies, remote signals or barrier semaphores. Data moves between devices by JAX's collectives and lax.ppermute only.
A program may use at most 64 MiB of HBM per device.

```python
import jax
import jax.numpy as jnp
from jax import lax

FIELDS = 8
NX = 1024
NY = 1024
RANK = 128
NZ = 2
STEPS = 2


def levels(own_key, shape, pieces, smallest, largest):
    def one(dim, parts):
        heights = jax.random.uniform(jax.random.fold_in(jax.random.fold_in(own_key, 6), dim), (parts,), jnp.float32, smallest / len(pieces), largest / len(pieces))
        return jnp.repeat(jnp.exp(heights), shape[dim] // parts).reshape((-1,) + (1,) * (len(shape) - dim - 1))

    loudness = one(*pieces[0])
    for cut in pieces[1:]:
        loudness = loudness * one(*cut)
    return loudness


def gaussian(rng, dims, spread, most, cuts=(), held_as=jnp.bfloat16):
    gain = levels(rng, dims, cuts, -0.22, 0.18) if cuts else 1.0
    result = jax.random.normal(rng, dims, jnp.float32) * spread * gain
    return jnp.minimum(jnp.maximum(result, -most), most).astype(held_as)


def setup_inputs(seed: int = 0) -> dict:
    key_list = jax.random.split(jax.random.key(seed), 7)
    fields = gaussian(key_list[0], (FIELDS, NZ, NX, NY), 1.0, 6.0, ((2, 2), (3, 16)), jnp.float32)
    diffusivity = jnp.clip(jax.random.uniform(key_list[1], (FIELDS,), jnp.float32, 0.03, 0.12), 0.03, 0.12)
    velocity = jnp.clip(jax.random.uniform(key_list[2], (2, FIELDS), jnp.float32, -0.4, 0.4), -0.4, 0.4)
    coupling = gaussian(key_list[3], (FIELDS, FIELDS), 0.15, 0.6, (), jnp.float32)
    basis_x = gaussian(key_list[4], (NX, RANK), NX ** -0.5, 0.1875)
    basis_y = gaussian(key_list[5], (NY, RANK), NY ** -0.5, 0.1875)
    return dict(fields=fields, diffusivity=diffusivity, velocity=velocity, coupling=coupling, basis_x=basis_x, basis_y=basis_y)


time_step = 1.0


def rates(state, diffusivity, velocity, coupling):
    lapl = -6.0 * state
    for axis_id in (1, 2, 3):
        lapl = lapl + jnp.roll(state, 1, axis_id) + jnp.roll(state, -1, axis_id)
    grad_x = (jnp.roll(state, -1, 2) - jnp.roll(state, 1, 2)) * 0.5
    grad_y = (jnp.roll(state, -1, 3) - jnp.roll(state, 1, 3)) * 0.5
    react = jnp.einsum("fg,gzxy->fzxy", coupling, jnp.tanh(state), precision=lax.Precision.HIGHEST)
    return (diffusivity[:, None, None, None] * lapl
            - velocity[0][:, None, None, None] * grad_x
            - velocity[1][:, None, None, None] * grad_y + react)


def reference(fields, diffusivity, velocity, coupling, basis_x, basis_y):
    state = fields
    for repeat in range(STEPS):
        first = rates(state, diffusivity, velocity, coupling)
        second = rates(state + 0.5 * time_step * first, diffusivity, velocity, coupling)
        third = rates(state + 0.5 * time_step * second, diffusivity, velocity, coupling)
        fourth = rates(state + time_step * third, diffusivity, velocity, coupling)
        state = state + (time_step / 6.0) * (first + 2.0 * second + 2.0 * third + fourth)
    unfold_x = jnp.transpose(state, (2, 0, 1, 3)).reshape(NX, -1)
    gram_x = jnp.dot(unfold_x, unfold_x.T, precision=lax.Precision.HIGHEST) / (FIELDS * NZ * NY)
    projected = jnp.einsum("xr,fzxy->fzry", basis_x.astype(jnp.float32), state, precision=lax.Precision.HIGHEST)
    unfold_y = jnp.transpose(projected, (3, 0, 1, 2)).reshape(NY, -1)
    gram_y = jnp.dot(unfold_y, unfold_y.T, precision=lax.Precision.HIGHEST) / (FIELDS * NZ * RANK)
    core = jnp.einsum("ys,fzry->fzrs", basis_y.astype(jnp.float32), projected, precision=lax.Precision.HIGHEST)
    return state, gram_x, gram_y, core
```

```python
import functools
import jax
import jax.numpy as jnp
from jax import lax
from jax.experimental import pallas as pl
from jax.experimental.pallas import tpu as pltpu
from jax.sharding import PartitionSpec as P

STEPS = 2
LANES = 128
time_step = 1.0


def pack_edges(fields_t, halo):
    nfield, depth, ycols, xrows = fields_t.shape
    first = min(xrows, LANES)

    def kernel(u_ref, head_ref, tail_ref):
        lane = lax.broadcasted_iota(jnp.int32, (ycols, LANES), 1)
        head = jnp.zeros((ycols, LANES), jnp.float32)
        tail = jnp.zeros((ycols, LANES), jnp.float32)
        for z in range(depth):
            for f in range(nfield):
                at = (z * nfield + f) * halo
                left = u_ref[f, z, :, 0:first]
                right = u_ref[f, z, :, xrows - first:xrows]
                if first < LANES:
                    fill = jnp.zeros((ycols, LANES - first), jnp.float32)
                    left = jnp.concatenate([left, fill], 1)
                    right = jnp.concatenate([right, fill], 1)
                mine = (lane >= at) & (lane < at + halo)
                head = jnp.where(mine, pltpu.roll(left, at, 1) if at else left, head)
                shift = (at - (first - halo)) % LANES
                tail = jnp.where(mine, pltpu.roll(right, shift, 1) if shift else right, tail)
        head_ref[...] = head
        tail_ref[...] = tail

    shape = jax.ShapeDtypeStruct((ycols, LANES), jnp.float32)
    return pl.pallas_call(kernel, out_shape=(shape, shape), name="pack_edges")(fields_t)


def stencil_steps(fields_t, y_before, y_after, x_before, x_after, coef, mix, halo):
    nfield, depth, ycols, xrows = fields_t.shape
    wide = ycols + 2 * halo
    lanes = -(-(xrows + 2 * halo) // LANES) * LANES
    tiles = lanes // LANES
    whole = xrows // LANES
    span = mix.shape[0] // (2 * depth * nfield)
    rows = depth * span * nfield
    stages = 4

    def kernel(u_ref, yb_ref, ya_ref, xb_ref, xa_ref, coef_ref, mix_ref, out_ref, u, p, q, acc, tcat, react):
        lane = lax.broadcasted_iota(jnp.int32, (halo, LANES), 1)

        def put(row, f, z, tile, value):
            n = value.shape[0]
            u[tile, pl.ds((z * wide + row) * nfield + f, n, stride=nfield), :] = value

        def edge(f, z, row, part):
            at = (z * nfield + f) * halo
            n = part.shape[0] if part is not None else None
            start = xrows - whole * LANES
            xa = xa_ref[pl.ds(row, halo), :]
            xb = xb_ref[pl.ds(row, halo), :]
            sa = (start - at) % LANES
            sb = (LANES - halo - at) % LANES
            xa = pltpu.roll(xa, sa, 1) if sa else xa
            xb = pltpu.roll(xb, sb, 1) if sb else xb
            base = jnp.zeros((halo, LANES), jnp.float32)
            if part is not None:
                base = jnp.concatenate([part, jnp.zeros((halo, LANES - start), jnp.float32)], 1)
            value = jnp.where((lane >= start) & (lane < start + halo), xa, base)
            return jnp.where(lane >= LANES - halo, xb, value)

        for z in range(depth):
            for f in range(nfield):
                for source, row, n in ((yb_ref, 0, halo), (u_ref, halo, ycols), (ya_ref, halo + ycols, halo)):
                    for tile in range(whole):
                        put(row, f, z, tile, source[f, z, :, tile * LANES:(tile + 1) * LANES])
                    for r in range(0, n, halo):
                        part = None
                        if xrows > whole * LANES:
                            part = source[f, z, r:r + halo, whole * LANES:xrows]
                        put(row + r, f, z, tiles - 1, edge(f, z, row + r, part))

        column = lax.broadcasted_iota(jnp.int32, (nfield, LANES), 1)
        is_last = column == LANES - 1
        is_first = column == 0

        def place(z, row, n=1):
            return pl.ds(pl.multiple_of((z * wide + row) * nfield, nfield), n * nfield)

        def prepare(src, row, slot):
            for z in range(depth):
                for r in range(0, span, 2):
                    for tile in range(tiles):
                        t = jnp.tanh(src[tile, place(z, row + r, 2), :])
                        hi = t.astype(jnp.bfloat16)
                        lo = (t - hi.astype(jnp.float32)).astype(jnp.bfloat16)
                        k = (z * span + r) * nfield
                        cols = slice(tile * LANES, (tile + 1) * LANES)
                        tcat[slot, k:k + 2 * nfield, cols] = hi
                        tcat[slot, rows + k:rows + k + 2 * nfield, cols] = lo

        def stage(which, src, dst, first, count):
            c = [coef_ref[i] for i in range(6)]
            last = wide - 1 - span
            prepare(src, first, 0)

            def body(g, carry):
                slot = lax.rem(g, 2)
                row = jnp.minimum(first + g * span, last)
                nxt = jnp.minimum(first + (g + 1) * span, last)
                both = jnp.dot(mix_ref[...], tcat[slot], preferred_element_type=jnp.float32)
                react[...] = both[:rows] + both[rows:]
                prepare(src, nxt, 1 - slot)
                for z in range(depth):
                    for r in range(span):
                        k = (z * span + r) * nfield
                        here = place(z, row + r)
                        mids = [src[tile, here, :] for tile in range(tiles)]
                        ups = [pltpu.roll(m, LANES - 1, 1) for m in mids]
                        downs = [pltpu.roll(m, 1, 1) for m in mids]
                        for tile in range(tiles):
                            mid = mids[tile]
                            h = react[k:k + nfield, tile * LANES:(tile + 1) * LANES] + c[0] * mid
                            if depth == 2:
                                h = h + c[1] * src[tile, place(1 - z, row + r), :]
                            else:
                                h = h + (0.5 * c[1]) * (src[tile, place((z + 1) % depth, row + r), :]
                                                        + src[tile, place((z - 1) % depth, row + r), :])
                            h = h + c[2] * src[tile, place(z, row + r + 1), :] + c[3] * src[tile, place(z, row + r - 1), :]
                            h = h + c[4] * jnp.where(is_last, ups[(tile + 1) % tiles], ups[tile])
                            h = h + c[5] * jnp.where(is_first, downs[(tile - 1) % tiles], downs[tile])
                            if which == 0:
                                dst[tile, here, :] = mid + h
                            elif which == 1:
                                y = u[tile, here, :] + h
                                dst[tile, here, :] = y
                                acc[tile, here, :] = mid + y + h
                            elif which == 2:
                                dst[tile, here, :] = u[tile, here, :] + (h + h)
                            else:
                                dst[tile, here, :] = (acc[tile, here, :] + mid + h) * (1.0 / 3.0)
                return carry

            lax.fori_loop(0, count, body, 0)

        for buffer in (p, q):
            for z in range(depth):
                for row in (0, wide - 1):
                    for tile in range(tiles):
                        buffer[tile, place(z, row), :] = jnp.zeros((nfield, LANES), jnp.float32)

        for step in range(STEPS):
            for which in range(stages):
                reach = halo - (step * stages + which) - 1
                first = halo - reach
                count = -(-(ycols + 2 * reach) // span)
                src = (u, p, q, p)[which]
                dst = (p, q, p, u)[which]
                stage(which, src, dst, first, count)
        for z in range(depth):
            for f in range(nfield):
                kept = pl.ds((z * wide + halo) * nfield + f, ycols, stride=nfield)
                for tile in range(whole):
                    out_ref[f, z, :, tile * LANES:(tile + 1) * LANES] = u[tile, kept, :]
                if xrows > whole * LANES:
                    out_ref[f, z, :, whole * LANES:xrows] = u[whole, kept, :][:, :xrows - whole * LANES]

    state = pltpu.VMEM((tiles, depth * wide * nfield, LANES), jnp.float32)
    return pl.pallas_call(
        kernel,
        out_shape=jax.ShapeDtypeStruct(fields_t.shape, jnp.float32),
        scratch_shapes=[state, state, state, state,
                        pltpu.VMEM((2, 2 * rows, lanes), jnp.bfloat16),
                        pltpu.VMEM((rows, lanes), jnp.float32)],
        compiler_params=pltpu.CompilerParams(vmem_limit_bytes=48 << 20),
        name="stencil_steps",
    )(fields_t, y_before, y_after, x_before, x_after, coef, mix)


def prepare_coefficients(diffusivity, velocity, coupling, depth):
    nfield = diffusivity.shape[0]
    half = 0.5 * time_step
    d = half * diffusivity
    vx = (0.5 * half) * velocity[0]
    vy = (0.5 * half) * velocity[1]
    coef = jnp.stack([-6.0 * d, 2.0 * d, d - vy, d + vy, d - vx, d + vx])
    coef = jnp.broadcast_to(coef[:, :, None], (6, nfield, LANES))
    span = max(2, LANES // (depth * nfield))
    c = half * coupling
    hi = lax.reduce_precision(c, 8, 7)
    lo = lax.reduce_precision(c - hi, 8, 7)
    eye = jnp.eye(depth * span, dtype=jnp.float32)
    def block(m):
        return (eye[:, None, :, None] * m[None, :, None, :]).reshape(depth * span * nfield, depth * span * nfield)
    hi, lo = block(hi), block(lo)
    mix = jnp.concatenate([jnp.concatenate([hi, hi], 1), jnp.concatenate([lo, lo], 1)], 0).astype(jnp.bfloat16)
    return coef, mix


highest = lax.Precision.HIGHEST


def ring(sizes, offsets):
    pairs = []
    total = 1
    for n in sizes:
        total *= n
    for i in range(total):
        rest, place = i, []
        for n in reversed(sizes):
            place.append(rest % n)
            rest //= n
        j = 0
        for p, o, n in zip(reversed(place), offsets, sizes):
            j = j * n + (p + o) % n
        pairs.append((i, j))
    return pairs


def halos(fields_t, halo):
    axes = ("sim", "grp", "gz")
    sizes = (lax.axis_size("sim"), lax.axis_size(("grp", "gz")))
    ycols = fields_t.shape[2]

    def send(part, over_x, over_y):
        return lax.ppermute(part, axes, ring(sizes, (over_x, over_y)))

    low, high = fields_t[:, :, :halo], fields_t[:, :, ycols - halo:]
    y_before = send(high, 0, 1)
    y_after = send(low, 0, -1)
    head, tail = pack_edges(fields_t, halo)
    x_before = jnp.concatenate([send(tail[ycols - halo:], 1, 1), send(tail, 1, 0), send(tail[:halo], 1, -1)], 0)
    x_after = jnp.concatenate([send(head[ycols - halo:], -1, 1), send(head, -1, 0), send(head[:halo], -1, -1)], 0)
    return y_before, y_after, x_before, x_after


def shards(fields, diffusivity, velocity, coupling, basis_x, basis_y):
    halo = 4 * STEPS
    depth = fields.shape[1]
    nfield = fields.shape[0]
    ycols_all = fields.shape[3] * lax.axis_size(("grp", "gz"))
    rank = basis_y.shape[1]
    fields_t = jnp.transpose(fields, (0, 1, 3, 2))
    coef, mix = prepare_coefficients(diffusivity, velocity, coupling, depth)
    edges = halos(fields_t, halo)
    state = stencil_steps(fields_t, *edges, coef, mix, halo)
    state = jnp.transpose(state, (0, 1, 3, 2))
    x_rows = state.shape[2]
    basis_xf = basis_x.astype(jnp.float32)
    basis_yf = basis_y.astype(jnp.float32)
    gram_rows = jnp.einsum(
        "fzxy,fzwy->xw", state, lax.all_gather(state, "sim", axis=2, tiled=True), precision=highest
    )
    own_basis = lax.dynamic_slice_in_dim(basis_xf, lax.axis_index("sim") * x_rows, x_rows, 0)
    partial_proj = jnp.einsum("xr,fzxy->fzry", own_basis, state, precision=highest)
    projected = lax.psum_scatter(partial_proj, "sim", scatter_dimension=2, tiled=True)
    gram_x = lax.psum_scatter(gram_rows, ("grp", "gz"), scatter_dimension=1, tiled=True) / (
        nfield * depth * ycols_all
    )
    rank_grp = rank // lax.axis_size(("grp", "gz"))
    rank_cols_y = lax.dynamic_slice_in_dim(
        basis_yf, lax.axis_index(("grp", "gz")) * rank_grp, rank_grp, 1
    )
    incoming = lax.all_gather(projected, ("grp", "gz"), axis=3, tiled=True)
    block = jnp.einsum("fzry,fzrv->yv", projected, incoming, precision=highest)
    core_part = jnp.einsum("vs,fzrv->fzrs", rank_cols_y, incoming, precision=highest)
    gram_y = lax.psum_scatter(block, "sim", scatter_dimension=1, tiled=True) / (nfield * depth * rank)
    return (state, gram_x, gram_y, core_part)


def solution(mesh):
    in_specs = (P(None, None, "sim", ("grp", "gz")), P(), P(), P(), P(), P())
    out_specs = (
        P(None, None, "sim", ("grp", "gz")),
        P("sim", ("grp", "gz")),
        P(("grp", "gz"), "sim"),
        P(None, None, "sim", ("grp", "gz")),
    )
    return jax.shard_map(shards, mesh=mesh, in_specs=in_specs, out_specs=out_specs, check_vma=False)
```

```python
import functools
import jax
import jax.numpy as jnp
from jax import lax
from jax.experimental import pallas as pl
from jax.experimental.pallas import tpu as pltpu
from jax.sharding import PartitionSpec as P

STEPS = 2
LANES = 128
time_step = 1.0


def pack_edges(fields_t, halo):
    nfield, depth, ycols, xrows = fields_t.shape
    first = min(xrows, LANES)

    def kernel(u_ref, head_ref, tail_ref):
        lane = lax.broadcasted_iota(jnp.int32, (ycols, LANES), 1)
        head = jnp.zeros((ycols, LANES), jnp.float32)
        tail = jnp.zeros((ycols, LANES), jnp.float32)
        for z in range(depth):
            for f in range(nfield):
                at = (z * nfield + f) * halo
                left = u_ref[f, z, :, 0:first]
                right = u_ref[f, z, :, xrows - first:xrows]
                if first < LANES:
                    fill = jnp.zeros((ycols, LANES - first), jnp.float32)
                    left = jnp.concatenate([left, fill], 1)
                    right = jnp.concatenate([right, fill], 1)
                mine = (lane >= at) & (lane < at + halo)
                head = jnp.where(mine, pltpu.roll(left, at, 1) if at else left, head)
                shift = (at - (first - halo)) % LANES
                tail = jnp.where(mine, pltpu.roll(right, shift, 1) if shift else right, tail)
        head_ref[...] = head
        tail_ref[...] = tail

    shape = jax.ShapeDtypeStruct((ycols, LANES), jnp.float32)
    return pl.pallas_call(kernel, out_shape=(shape, shape), name="pack_edges")(fields_t)


def stencil_steps(fields_t, y_before, y_after, x_before, x_after, coef, mix, halo):
    nfield, depth, ycols, xrows = fields_t.shape
    wide = ycols + 2 * halo
    lanes = -(-(xrows + 2 * halo) // LANES) * LANES
    tiles = lanes // LANES
    whole = xrows // LANES
    span = mix.shape[0] // (2 * depth * nfield)
    rows = depth * span * nfield
    stages = 4

    def kernel(u_ref, yb_ref, ya_ref, xb_ref, xa_ref, coef_ref, mix_ref, out_ref, u, p, q, acc, tcat, react):
        lane = lax.broadcasted_iota(jnp.int32, (halo, LANES), 1)

        def put(row, f, z, tile, value):
            n = value.shape[0]
            u[tile, pl.ds((z * wide + row) * nfield + f, n, stride=nfield), :] = value

        def edge(f, z, row, part):
            at = (z * nfield + f) * halo
            n = part.shape[0] if part is not None else None
            start = xrows - whole * LANES
            xa = xa_ref[pl.ds(row, halo), :]
            xb = xb_ref[pl.ds(row, halo), :]
            sa = (start - at) % LANES
            sb = (LANES - halo - at) % LANES
            xa = pltpu.roll(xa, sa, 1) if sa else xa
            xb = pltpu.roll(xb, sb, 1) if sb else xb
            base = jnp.zeros((halo, LANES), jnp.float32)
            if part is not None:
                base = jnp.concatenate([part, jnp.zeros((halo, LANES - start), jnp.float32)], 1)
            value = jnp.where((lane >= start) & (lane < start + halo), xa, base)
            return jnp.where(lane >= LANES - halo, xb, value)

        for z in range(depth):
            for f in range(nfield):
                for source, row, n in ((yb_ref, 0, halo), (u_ref, halo, ycols), (ya_ref, halo + ycols, halo)):
                    for tile in range(whole):
                        put(row, f, z, tile, source[f, z, :, tile * LANES:(tile + 1) * LANES])
                    for r in range(0, n, halo):
                        part = None
                        if xrows > whole * LANES:
                            part = source[f, z, r:r + halo, whole * LANES:xrows]
                        put(row + r, f, z, tiles - 1, edge(f, z, row + r, part))

        column = lax.broadcasted_iota(jnp.int32, (nfield, LANES), 1)
        is_last = column == LANES - 1
        is_first = column == 0

        def place(z, row, n=1):
            return pl.ds(pl.multiple_of((z * wide + row) * nfield, nfield), n * nfield)

        def prepare(src, row, slot):
            for z in range(depth):
                for r in range(0, span, 2):
                    for tile in range(tiles):
                        t = jnp.tanh(src[tile, place(z, row + r, 2), :])
                        hi = t.astype(jnp.bfloat16)
                        lo = (t - hi.astype(jnp.float32)).astype(jnp.bfloat16)
                        k = (z * span + r) * nfield
                        cols = slice(tile * LANES, (tile + 1) * LANES)
                        tcat[slot, k:k + 2 * nfield, cols] = hi
                        tcat[slot, rows + k:rows + k + 2 * nfield, cols] = lo

        def stage(which, src, dst, first, count):
            c = [coef_ref[i] for i in range(6)]
            last = wide - 1 - span
            prepare(src, first, 0)

            def body(g, carry):
                slot = lax.rem(g, 2)
                row = jnp.minimum(first + g * span, last)
                nxt = jnp.minimum(first + (g + 1) * span, last)
                both = jnp.dot(mix_ref[...], tcat[slot], preferred_element_type=jnp.float32)
                react[...] = both[:rows] + both[rows:]
                prepare(src, nxt, 1 - slot)
                for z in range(depth):
                    for r in range(span):
                        k = (z * span + r) * nfield
                        here = place(z, row + r)
                        mids = [src[tile, here, :] for tile in range(tiles)]
                        ups = [pltpu.roll(m, LANES - 1, 1) for m in mids]
                        downs = [pltpu.roll(m, 1, 1) for m in mids]
                        for tile in range(tiles):
                            mid = mids[tile]
                            h = react[k:k + nfield, tile * LANES:(tile + 1) * LANES] + c[0] * mid
                            if depth == 2:
                                h = h + c[1] * src[tile, place(1 - z, row + r), :]
                            else:
                                h = h + (0.5 * c[1]) * (src[tile, place((z + 1) % depth, row + r), :]
                                                        + src[tile, place((z - 1) % depth, row + r), :])
                            h = h + c[2] * src[tile, place(z, row + r + 1), :] + c[3] * src[tile, place(z, row + r - 1), :]
                            h = h + c[4] * jnp.where(is_last, ups[(tile + 1) % tiles], ups[tile])
                            h = h + c[5] * jnp.where(is_first, downs[(tile - 1) % tiles], downs[tile])
                            if which == 0:
                                dst[tile, here, :] = mid + h
                            elif which == 1:
                                y = u[tile, here, :] + h
                                dst[tile, here, :] = y
                                acc[tile, here, :] = mid + y + h
                            elif which == 2:
                                dst[tile, here, :] = u[tile, here, :] + (h + h)
                            else:
                                dst[tile, here, :] = (acc[tile, here, :] + mid + h) * (1.0 / 3.0)
                return carry

            lax.fori_loop(0, count, body, 0)

        for buffer in (p, q):
            for z in range(depth):
                for row in (0, wide - 1):
                    for tile in range(tiles):
                        buffer[tile, place(z, row), :] = jnp.zeros((nfield, LANES), jnp.float32)

        for step in range(STEPS):
            for which in range(stages):
                reach = halo - (step * stages + which) - 1
                first = halo - reach
                count = -(-(ycols + 2 * reach) // span)
                src = (u, p, q, p)[which]
                dst = (p, q, p, u)[which]
                stage(which, src, dst, first, count)
        for z in range(depth):
            for f in range(nfield):
                kept = pl.ds((z * wide + halo) * nfield + f, ycols, stride=nfield)
                for tile in range(whole):
                    out_ref[f, z, :, tile * LANES:(tile + 1) * LANES] = u[tile, kept, :]
                if xrows > whole * LANES:
                    out_ref[f, z, :, whole * LANES:xrows] = u[whole, kept, :][:, :xrows - whole * LANES]

    state = pltpu.VMEM((tiles, depth * wide * nfield, LANES), jnp.float32)
    return pl.pallas_call(
        kernel,
        out_shape=jax.ShapeDtypeStruct(fields_t.shape, jnp.float32),
        scratch_shapes=[state, state, state, state,
                        pltpu.VMEM((2, 2 * rows, lanes), jnp.bfloat16),
                        pltpu.VMEM((rows, lanes), jnp.float32)],
        compiler_params=pltpu.CompilerParams(vmem_limit_bytes=48 << 20),
        name="stencil_steps",
    )(fields_t, y_before, y_after, x_before, x_after, coef, mix)


def prepare_coefficients(diffusivity, velocity, coupling, depth):
    nfield = diffusivity.shape[0]
    half = 0.5 * time_step
    d = half * diffusivity
    vx = (0.5 * half) * velocity[0]
    vy = (0.5 * half) * velocity[1]
    coef = jnp.stack([-6.0 * d, 2.0 * d, d - vy, d + vy, d - vx, d + vx])
    coef = jnp.broadcast_to(coef[:, :, None], (6, nfield, LANES))
    span = max(2, LANES // (depth * nfield))
    c = half * coupling
    hi = lax.reduce_precision(c, 8, 7)
    lo = lax.reduce_precision(c - hi, 8, 7)
    eye = jnp.eye(depth * span, dtype=jnp.float32)
    def block(m):
        return (eye[:, None, :, None] * m[None, :, None, :]).reshape(depth * span * nfield, depth * span * nfield)
    hi, lo = block(hi), block(lo)
    mix = jnp.concatenate([jnp.concatenate([hi, hi], 1), jnp.concatenate([lo, lo], 1)], 0).astype(jnp.bfloat16)
    return coef, mix


high = lax.Precision.HIGH
highest = lax.Precision.HIGHEST
AXES = ("sim", "grp", "gz")


def ring(sizes, offsets):
    pairs = []
    for i in range(sizes[0]):
        for j in range(sizes[1]):
            pairs.append((i * sizes[1] + j, (i + offsets[0]) % sizes[0] * sizes[1] + (j + offsets[1]) % sizes[1]))
    return pairs


def halos(fields_t, head, tail, halo):
    sizes = (lax.axis_size("sim"), lax.axis_size(("grp", "gz")))
    ycols = fields_t.shape[2]

    def send(part, over_x, over_y):
        return lax.ppermute(part, AXES, ring(sizes, (over_x, over_y)))

    low, high_ = fields_t[:, :, :halo], fields_t[:, :, ycols - halo:]
    if sizes[0] == 2:
        both = send(jnp.concatenate([head, tail], 1), 1, 0)
        x_after, x_before = both[:, :LANES], both[:, LANES:]
    else:
        x_before, x_after = send(tail, 1, 0), send(head, -1, 0)
    pad = fields_t.shape[3]
    corner = jnp.concatenate([x_before, x_after], 1)
    if pad < 2 * LANES:
        y_before, y_after = send(high_, 0, 1), send(low, 0, -1)
        up, down = send(corner[ycols - halo:], 0, 1), send(corner[:halo], 0, -1)
    else:
        corner = jnp.pad(corner, ((0, 0), (0, pad - 2 * LANES)))
        rows = low.size // pad

        def joined(part, edge, over_y):
            moved = send(jnp.concatenate([part.reshape(rows, pad), edge], 0), 0, over_y)
            return moved[:rows].reshape(part.shape), moved[rows:, :2 * LANES]

        y_before, up = joined(high_, corner[ycols - halo:], 1)
        y_after, down = joined(low, corner[:halo], -1)
    x_before = jnp.concatenate([up[:, :LANES], x_before, down[:, :LANES]], 0)
    x_after = jnp.concatenate([up[:, LANES:], x_after, down[:, LANES:]], 0)
    return y_before, y_after, x_before, x_after


def gram_messages(gathered, basis_cols, place):
    n_core, n_grp, n_pair, nf, ycols, rank = gathered.shape
    count = n_core * n_grp * n_pair * ycols
    half = count // 2
    ncols = basis_cols.shape[0] // n_pair
    wide = nf * rank

    def kernel(place_ref, q_ref, by_ref, out_ref, hi, lo, res):
        s, z, x, c = (place_ref[i] for i in range(4))
        for zz in range(n_grp):
            for xx in range(n_pair):
                for cc in range(n_core):
                    row = ((zz * n_pair + xx) * n_core + cc) * ycols
                    for f in range(nf):
                        q = q_ref[cc ^ c, zz ^ z, xx, f]
                        big = q.astype(jnp.bfloat16)
                        hi[row:row + ycols, f * rank:(f + 1) * rank] = big
                        lo[row:row + ycols, f * rank:(f + 1) * rank] = (q - big.astype(jnp.float32)).astype(jnp.bfloat16)
        dims = (((1,), (1,)), ((), ()))
        for dx in range(n_pair):
            row = pl.multiple_of(((z * n_pair + (x ^ dx)) * n_core + c) * ycols, ycols)
            mine_hi = hi[pl.ds(row, ycols), :]
            mine_lo = lo[pl.ds(row, ycols), :]
            for side in range(2):
                cols = slice(side * half, (side + 1) * half)
                part = lax.dot_general(mine_hi, hi[cols, :], dims, preferred_element_type=jnp.float32)
                part += lax.dot_general(mine_lo, hi[cols, :], dims, preferred_element_type=jnp.float32)
                part += lax.dot_general(mine_hi, lo[cols, :], dims, preferred_element_type=jnp.float32)
                out_ref[dx, side ^ s, 0:ycols, :] = part
        core = jnp.dot(by_ref[...], hi[...], preferred_element_type=jnp.float32)
        core += jnp.dot(by_ref[...], lo[...], preferred_element_type=jnp.float32)
        res[...] = core
        keep = rank // 2
        for dx in range(n_pair):
            mine = res[pl.ds(pl.multiple_of((x ^ dx) * ncols, ncols), ncols), :]
            for side in range(2):
                parts = [mine[:, f * rank + side * keep:f * rank + (side + 1) * keep] for f in range(nf)]
                parts.append(jnp.zeros((ncols, half - nf * keep), jnp.float32))
                out_ref[dx, side ^ s, ycols:ycols + ncols, :] = jnp.concatenate(parts, 1)

    return pl.pallas_call(
        kernel,
        in_specs=[pl.BlockSpec(memory_space=pltpu.SMEM)] + [pl.BlockSpec(memory_space=pltpu.VMEM)] * 2,
        out_shape=jax.ShapeDtypeStruct((n_pair, 2, ycols + ncols, half), jnp.float32),
        scratch_shapes=[pltpu.VMEM((count, wide), jnp.bfloat16)] * 2 + [pltpu.VMEM((n_pair * ncols, wide), jnp.float32)],
        compiler_params=pltpu.CompilerParams(vmem_limit_bytes=32 << 20),
        cost_estimate=pl.CostEstimate(flops=6 * 2 * ycols * count * wide, bytes_accessed=8 * count * wide, transcendentals=0),
        name="gram_messages",
    )(place, gathered, basis_cols)


def finish_y(pieces, place, nf, ycols, scale):
    rows, half = pieces[0].shape
    ncols = rows - ycols

    def kernel(place_ref, a_ref, b_ref, c_ref, d_ref, gram_ref, core_ref):
        s, x = place_ref[0], place_ref[2]
        refs = (a_ref, b_ref, c_ref, d_ref)
        gram_ref[...] = ((a_ref[0:ycols, :] + b_ref[0:ycols, :]) + (c_ref[0:ycols, :] + d_ref[0:ycols, :])) * scale
        r = core_ref.shape[3]
        for dx in range(2):
            for ds in range(2):
                piece = refs[2 * dx + ds][ycols:rows, :]
                for f in range(nf):
                    core_ref[(x ^ dx) * nf + f, s ^ ds] = piece[:, f * r:(f + 1) * r]

    def call(r):
        return pl.pallas_call(
            kernel,
            in_specs=[pl.BlockSpec(memory_space=pltpu.SMEM)] + [pl.BlockSpec(memory_space=pltpu.VMEM)] * 4,
            out_shape=(jax.ShapeDtypeStruct((ycols, half), jnp.float32),
                       jax.ShapeDtypeStruct((2 * nf, 2, ncols, r), jnp.float32)),
            name="finish_y",
        )(place, *pieces)

    return call


def pairwise(state_t, basis_x, basis_y):
    n_grp, n_gz = lax.axis_size("grp"), lax.axis_size("gz")
    nfield, depth, ycols, xrows = state_t.shape
    rank = basis_x.shape[1]
    size = 2 * n_grp * n_gz
    core_bit, pair_bit, near_bit, far_bit, sim_bit = 1, n_gz // 2, n_gz, 2 * n_gz, n_grp * n_gz
    s, z, gz = lax.axis_index("sim"), lax.axis_index("grp"), lax.axis_index("gz")
    x, c = gz // 2, gz % 2
    place = jnp.stack([s, z, x, c]).astype(jnp.int32)

    def swap(part, bits, name):
        with jax.named_scope(name):
            return lax.ppermute(part, AXES, [(i, i ^ bits) for i in range(size)])

    def pick(part, index, axis):
        return lax.dynamic_index_in_dim(part, index, axis, keepdims=False)

    other = swap(state_t, sim_bit, "exchange")

    def project(part, side):
        rows = lax.dynamic_slice_in_dim(basis_x, side * xrows, xrows, 0).astype(jnp.float32)
        return jnp.einsum("fyx,xr->fyr", pick(part, s, 1), rows, precision=high)

    proj = project(state_t, s) + project(other, 1 - s)
    proj = proj.reshape(2, nfield // 2, ycols, rank)
    mine, theirs = pick(proj, x, 0), swap(pick(proj, 1 - x, 0), pair_bit, "q_pair")
    pair = jnp.where(x == 0, jnp.stack([mine, theirs]), jnp.stack([theirs, mine]))
    near = swap(pair, near_bit, "q_near")
    far = swap(pair, far_bit, "q_far")
    both = swap(far, near_bit, "q_both")
    chip = jnp.stack([pair, near, far, both])
    gathered = jnp.stack([chip, swap(chip, core_bit, "q_core")])
    by = basis_y.T.reshape(n_grp, 2, 2, rank // (n_grp * n_gz), -1)
    by = pick(pick(by, c, 2), z, 0).reshape(-1, basis_y.shape[0])
    messages = gram_messages(gathered, by, place)
    pieces = [messages[0, 0], swap(messages[0, 1], sim_bit, "y_sim"), swap(messages[1, 0], pair_bit, "y_pair"),
              swap(messages[1, 1], sim_bit | pair_bit, "y_diag")]
    gram_y, core = finish_y(pieces, place, nfield // 2, ycols, 1.0 / (nfield * depth * rank))(rank // 2)

    def fold(part):
        block = jnp.einsum("fzyw,fzyx->wx", part, state_t, precision=high).reshape(2, 2, 2, ycols, xrows)
        block = pick(block, c, 2) + swap(pick(block, 1 - c, 2), core_bit, "x_core")
        return pick(block, x, 1) + swap(pick(block, 1 - x, 1), pair_bit, "x_pair")

    same, cross = fold(state_t), fold(other)
    at_home = z // 2 == s
    kept = jnp.where(at_home, same, cross) + swap(jnp.where(at_home, cross, same), far_bit, "x_far")
    gram_x = pick(kept, z % 2, 0) + swap(pick(kept, 1 - z % 2, 0), near_bit, "x_near")
    gram_x = gram_x * (1.0 / (nfield * depth * ycols * n_grp * n_gz))
    return gram_x.T, gram_y, jnp.transpose(core, (0, 1, 3, 2))


def collective(state, basis_x, basis_y):
    nfield, depth, x_rows, ycols = state.shape
    rank = basis_y.shape[1]
    n_y = lax.axis_size(("grp", "gz"))
    basis_xf = basis_x.astype(jnp.float32)
    basis_yf = basis_y.astype(jnp.float32)
    gram_rows = jnp.einsum(
        "fzxy,fzwy->xw", state, lax.all_gather(state, "sim", axis=2, tiled=True), precision=highest
    )
    own_basis = lax.dynamic_slice_in_dim(basis_xf, lax.axis_index("sim") * x_rows, x_rows, 0)
    partial_proj = jnp.einsum("xr,fzxy->fzry", own_basis, state, precision=highest)
    projected = lax.psum_scatter(partial_proj, "sim", scatter_dimension=2, tiled=True)
    gram_x = lax.psum_scatter(gram_rows, ("grp", "gz"), scatter_dimension=1, tiled=True) / (
        nfield * depth * ycols * n_y
    )
    rank_grp = rank // n_y
    rank_cols_y = lax.dynamic_slice_in_dim(basis_yf, lax.axis_index(("grp", "gz")) * rank_grp, rank_grp, 1)
    incoming = lax.all_gather(projected, ("grp", "gz"), axis=3, tiled=True)
    block = jnp.einsum("fzry,fzrv->yv", projected, incoming, precision=highest)
    core_part = jnp.einsum("vs,fzrv->fzrs", rank_cols_y, incoming, precision=highest)
    gram_y = lax.psum_scatter(block, "sim", scatter_dimension=1, tiled=True) / (nfield * depth * rank)
    return gram_x, gram_y, core_part


def shards(fields, diffusivity, velocity, coupling, basis_x, basis_y):
    halo = 4 * STEPS
    depth = fields.shape[1]
    fields_t = jnp.transpose(fields, (0, 1, 3, 2))
    coef, mix = prepare_coefficients(diffusivity, velocity, coupling, depth)
    head, tail = pack_edges(fields_t, halo)
    edges = halos(fields_t, head, tail, halo)
    state_t = stencil_steps(fields_t, *edges, coef, mix, halo)
    state = jnp.transpose(state_t, (0, 1, 3, 2))
    sizes = tuple(lax.axis_size(a) for a in AXES)
    if sizes[0] == depth == 2 and sizes[1] == sizes[2] == 4:
        return (state, *pairwise(state_t, basis_x, basis_y))
    return (state, *collective(state, basis_x, basis_y))


def solution(mesh):
    in_specs = (P(None, None, "sim", ("grp", "gz")), P(), P(), P(), P(), P())
    out_specs = (
        P(None, None, "sim", ("grp", "gz")),
        P("sim", ("grp", "gz")),
        P(("grp", "gz"), "sim"),
        P(None, None, "sim", ("grp", "gz")),
    )
    return jax.shard_map(shards, mesh=mesh, in_specs=in_specs, out_specs=out_specs, check_vma=False)
```

```python
import jax
import jax.numpy as jnp
from jax import lax
from jax.experimental import pallas as pl
from jax.experimental.pallas import tpu as pltpu
from jax.sharding import PartitionSpec as P

STEPS = 2
STAGES = 4
LANES = 128
AXES = ("sim", "grp", "gz")
time_step = 1.0
high = lax.Precision.HIGH
highest = lax.Precision.HIGHEST


def setup(fields_t, diffusivity, velocity, coupling, halo, span):
    nfield, depth, ycols, xrows = fields_t.shape
    width = min(xrows, LANES)
    rows = depth * span * nfield
    half = 0.5 * time_step

    def kernel(first_ref, last_ref, d_ref, v_ref, c_ref, edge_ref, coef_ref, mix_ref):
        lane = lax.broadcasted_iota(jnp.int32, (ycols, LANES), 1)
        head = jnp.zeros((ycols, LANES), jnp.float32)
        tail = jnp.zeros((ycols, LANES), jnp.float32)
        for z in range(depth):
            for f in range(nfield):
                at = (z * nfield + f) * halo
                left, right = first_ref[f, z], last_ref[f, z]
                if width < LANES:
                    fill = jnp.zeros((ycols, LANES - width), jnp.float32)
                    left, right = jnp.concatenate([left, fill], 1), jnp.concatenate([right, fill], 1)
                mine = (lane >= at) & (lane < at + halo)
                head = jnp.where(mine, pltpu.roll(left, at, 1) if at else left, head)
                shift = (at - (width - halo)) % LANES
                tail = jnp.where(mine, pltpu.roll(right, shift, 1) if shift else right, tail)
        edge_ref[:, 0:LANES] = head
        edge_ref[:, LANES:2 * LANES] = tail
        sub = lax.broadcasted_iota(jnp.int32, (nfield, LANES), 0)

        def column(values):
            out = jnp.zeros((nfield, LANES), jnp.float32)
            for f in range(nfield):
                out = jnp.where(sub == f, values[f], out)
            return out

        d = column([d_ref[f] for f in range(nfield)]) * half
        vx = column([v_ref[0, f] for f in range(nfield)]) * (0.5 * half)
        vy = column([v_ref[1, f] for f in range(nfield)]) * (0.5 * half)
        for i, value in enumerate((-6.0 * d, 2.0 * d, d - vy, d + vy, d - vx, d + vx)):
            coef_ref[i] = value
        sub = lax.broadcasted_iota(jnp.int32, (nfield, rows), 0)
        mod = lax.broadcasted_iota(jnp.int32, (nfield, rows), 1) % nfield
        block = lax.broadcasted_iota(jnp.int32, (nfield, rows), 1) // nfield
        tile = jnp.zeros((nfield, rows), jnp.float32)
        for g in range(nfield):
            value = jnp.zeros((nfield, rows), jnp.float32)
            for f in range(nfield):
                value = jnp.where(sub == f, c_ref[f, g] * half, value)
            tile = jnp.where(mod == g, value, tile)
        hi = tile.astype(jnp.bfloat16).astype(jnp.float32)
        lo = tile - hi
        for part, base in ((hi, 0), (lo, rows)):
            for i in range(0, rows // nfield, 2):
                value = jnp.concatenate([jnp.where(block == i + k, part, 0.0) for k in range(2)], 0).astype(jnp.bfloat16)
                for j in range(2):
                    mix_ref[base + i * nfield:base + (i + 2) * nfield, j * rows:(j + 1) * rows] = value

    smem = pl.BlockSpec(memory_space=pltpu.SMEM)
    last = xrows // width - 1
    return pl.pallas_call(
        kernel,
        grid=(1,),
        in_specs=[pl.BlockSpec((nfield, depth, ycols, width), lambda i: (0, 0, 0, 0)),
                  pl.BlockSpec((nfield, depth, ycols, width), lambda i: (0, 0, 0, last)), smem, smem, smem],
        out_shape=(jax.ShapeDtypeStruct((ycols, 2 * LANES), jnp.float32),
                   jax.ShapeDtypeStruct((6, nfield, LANES), jnp.float32),
                   jax.ShapeDtypeStruct((2 * rows, 2 * rows), jnp.bfloat16)),
        out_specs=(pl.BlockSpec((ycols, 2 * LANES), lambda i: (0, 0)),
                   pl.BlockSpec((6, nfield, LANES), lambda i: (0, 0, 0)),
                   pl.BlockSpec((2 * rows, 2 * rows), lambda i: (0, 0))),
        name="setup",
    )(fields_t, fields_t, diffusivity, velocity, coupling)


def stencil_chunk(fields_t, blocks, carry, filled, coef, mix, side, halo, span, index, size, final):
    nfield, depth, ycols, xrows = fields_t.shape
    lanes = -(-(xrows + 2 * halo) // LANES) * LANES
    tiles = lanes // LANES
    whole = xrows // LANES
    rows = depth * span * nfield
    stages = STEPS * STAGES
    keep = halo + 1
    old = 0 if carry is None else keep
    win = old + halo * len(blocks)
    start = xrows - whole * LANES
    n = len(blocks)
    u, p, q, acc = range(4)
    joined_rows = -(-2 * LANES // xrows)

    def kernel(*refs):
        side_ref, refs = refs[0], refs[1:]
        sources, refs = refs[:n], refs[n:]
        edges = [None if b[2] is None else refs[0] for b in blocks]
        refs = refs[1:]
        carry_ref = None
        if carry is not None:
            carry_ref, _, refs = refs[0], refs[1], refs[2:]
        coef_ref, mix_ref, out_ref, give_ref, mine_ref = refs[:5]
        refs = refs[5:]
        left_ref = None
        if not final:
            left_ref, refs = refs[0], refs[1:]
        bufs, tcat, react = refs
        lane = lax.broadcasted_iota(jnp.int32, (halo, LANES), 1)
        column = lax.broadcasted_iota(jnp.int32, (nfield, LANES), 1)
        is_last = column == LANES - 1
        is_first = column == 0

        def place(z, row, count=1):
            return pl.ds(pl.multiple_of((z * win + row) * nfield, nfield), count * nfield)

        def strided(z, row, f, count):
            return pl.ds((z * win + row) * nfield + f, count, stride=nfield)

        def edge_of(i):
            if blocks[i][2] is None:
                parts = [sources[i][nfield * depth + k] for k in range(joined_rows)]
                both = parts[0] if joined_rows == 1 else jnp.concatenate(parts, 1)
            else:
                both = edges[i][blocks[i][3]:blocks[i][3] + halo, :]
            return both[:, 0:LANES], both[:, LANES:2 * LANES]

        for z in range(depth):
            if carry is not None:
                for b in range(4):
                    for tile in range(tiles):
                        bufs[b, tile, place(z, 0, keep), :] = carry_ref[b, tile, z]
            else:
                for b in (p, q):
                    for tile in range(tiles):
                        bufs[b, tile, place(z, 0), :] = jnp.zeros((nfield, LANES), jnp.float32)
            if final:
                for b in (p, q):
                    for tile in range(tiles):
                        bufs[b, tile, place(z, win - 1), :] = jnp.zeros((nfield, LANES), jnp.float32)
            for f in range(nfield):
                at = (z * nfield + f) * halo
                for i in range(n):
                    row = old + i * halo
                    whose = (f, z) if blocks[i][2] is not None else (f * depth + z,)
                    for tile in range(whole):
                        bufs[u, tile, strided(z, row, f, halo), :] = sources[i][(*whose, slice(None), slice(tile * LANES, (tile + 1) * LANES))]
                    after, before = edge_of(i)
                    sa, sb = (start - at) % LANES, (LANES - halo - at) % LANES
                    after = pltpu.roll(after, sa, 1) if sa else after
                    before = pltpu.roll(before, sb, 1) if sb else before
                    base = jnp.zeros((halo, LANES), jnp.float32)
                    if start:
                        part = sources[i][(*whose, slice(None), slice(whole * LANES, xrows))]
                        base = jnp.concatenate([part, jnp.zeros((halo, LANES - start), jnp.float32)], 1)
                    value = jnp.where((lane >= start) & (lane < start + halo), after, base)
                    bufs[u, tiles - 1, strided(z, row, f, halo), :] = jnp.where(lane >= LANES - halo, before, value)

        def prepare(src, row, slot):
            for z in range(depth):
                for r in range(0, span, 2):
                    for tile in range(tiles):
                        t = jnp.tanh(bufs[src, tile, place(z, row + r, 2), :])
                        hi = t.astype(jnp.bfloat16)
                        lo = (t - hi.astype(jnp.float32)).astype(jnp.bfloat16)
                        k = (z * span + r) * nfield
                        cols = slice(tile * LANES, (tile + 1) * LANES)
                        tcat[slot, k:k + 2 * nfield, cols] = hi
                        tcat[slot, rows + k:rows + k + 2 * nfield, cols] = lo

        def extent(k):
            low = keep - k if carry is not None else k
            top = win - k
            return top, (top - low + span - 1) // span

        def first_row(k):
            top, count = extent(k)
            return jnp.maximum(top - span * count, 1)

        def stage(which, k, slot):
            src, dst = (u, p, q, p)[which], (p, q, p, u)[which]
            c = [coef_ref[i] for i in range(6)]
            top, count = extent(k)
            following = first_row(jnp.minimum(k + 1, stages))

            def body(g, slot):
                row = jnp.maximum(top - span * (count - g), 1)
                ends = g == count - 1
                nxt = jnp.where(ends, following, jnp.maximum(top - span * (count - g - 1), 1))
                both = jnp.dot(mix_ref[...], tcat[slot], preferred_element_type=jnp.float32)
                react[...] = both[:rows] + both[rows:]
                for z in range(depth):
                    for r in range(span):
                        k = (z * span + r) * nfield
                        here = place(z, row + r)
                        mids = [bufs[src, tile, here, :] for tile in range(tiles)]
                        ups = [pltpu.roll(m, LANES - 1, 1) for m in mids]
                        downs = [pltpu.roll(m, 1, 1) for m in mids]
                        for tile in range(tiles):
                            mid = mids[tile]

                            def near(zz, rr):
                                return bufs[src, tile, place(zz % depth, row + rr), :]

                            h = react[k:k + nfield, tile * LANES:(tile + 1) * LANES] + c[0] * mid
                            if depth == 2:
                                h = h + c[1] * near(1 - z, r)
                            else:
                                h = h + (0.5 * c[1]) * (near(z + 1, r) + near(z - 1, r))
                            h = h + c[2] * near(z, r + 1) + c[3] * near(z, r - 1)
                            h = h + c[4] * jnp.where(is_last, ups[(tile + 1) % tiles], ups[tile])
                            h = h + c[5] * jnp.where(is_first, downs[(tile - 1) % tiles], downs[tile])
                            if which == 0:
                                bufs[dst, tile, here, :] = mid + h
                            elif which == 1:
                                y = bufs[u, tile, here, :] + h
                                bufs[dst, tile, here, :] = y
                                bufs[acc, tile, here, :] = mid + y + h
                            elif which == 2:
                                bufs[dst, tile, here, :] = bufs[u, tile, here, :] + (h + h)
                            else:
                                bufs[dst, tile, here, :] = (bufs[acc, tile, here, :] + mid + h) * (1.0 / 3.0)
                prepare(jnp.where(ends, dst, src), nxt, 1 - slot)
                return 1 - slot

            return lax.fori_loop(0, count, body, slot)

        prepare(u, first_row(1), 0)

        def step(i, slot):
            for which in range(STAGES):
                slot = stage(which, i * STAGES + which + 1, slot)
            return slot

        lax.fori_loop(0, STEPS, step, 0)
        bottom = win - halo - size
        s = side_ref[0]
        for f in range(nfield):
            for tile in range(whole + (start > 0)):
                width = LANES if tile < whole else start
                cols = slice(tile * LANES, tile * LANES + width)
                for z in range(depth):
                    out_ref[f, z, :, cols] = bufs[u, tile, strided(z, bottom, f, size), :][:, :width]
                give_ref[f, :, cols] = bufs[u, tile, strided((s + 1) % depth, bottom, f, size), :][:, :width]
                mine_ref[f, :, cols] = bufs[u, tile, strided(s % depth, bottom, f, size), :][:, :width]
        if not final:
            for z in range(depth):
                for b in range(4):
                    for tile in range(tiles):
                        left_ref[b, tile, z] = bufs[b, tile, place(z, win - keep, keep), :]

    vmem = pl.BlockSpec(memory_space=pltpu.VMEM)
    specs = [pl.BlockSpec(memory_space=pltpu.SMEM)]
    for array, at, edge, _ in blocks:
        if edge is None:
            specs.append(vmem)
        else:
            specs.append(pl.BlockSpec((nfield, depth, halo, xrows), (lambda i, at=at: (0, 0, at, 0))))
    specs.append(vmem)
    operands = [side, *(b[0] for b in blocks), next(b[2] for b in blocks if b[2] is not None)]
    aliases = {}
    if carry is not None:
        operands += [carry, filled]
        specs += [vmem, pl.BlockSpec(memory_space=pl.ANY)]
        aliases = {len(operands) - 1: 0}
    operands += [coef, mix]
    specs += [vmem, vmem]
    part = jax.ShapeDtypeStruct((nfield, size, xrows), jnp.float32)
    part_spec = pl.BlockSpec((nfield, size, xrows), lambda i: (0, 0, 0))
    shapes = [jax.ShapeDtypeStruct(fields_t.shape, jnp.float32), part, part]
    out_specs = [pl.BlockSpec((nfield, depth, size, xrows), lambda i: (0, 0, index, 0)), part_spec, part_spec]
    if not final:
        left = (4, tiles, depth, keep * nfield, LANES)
        shapes.append(jax.ShapeDtypeStruct(left, jnp.float32))
        out_specs.append(pl.BlockSpec(left, lambda i: (0, 0, 0, 0, 0)))
    work = sum(-(-(win - old - (0 if old else 2 * k)) // span) for k in range(1, stages + 1)) * rows * lanes
    return pl.pallas_call(
        kernel,
        grid=(1,),
        in_specs=specs,
        out_specs=out_specs,
        out_shape=shapes,
        scratch_shapes=[pltpu.VMEM((4, tiles, depth * win * nfield, LANES), jnp.float32),
                        pltpu.VMEM((2, 2 * rows, lanes), jnp.bfloat16),
                        pltpu.VMEM((rows, lanes), jnp.float32)],
        input_output_aliases=aliases,
        compiler_params=pltpu.CompilerParams(vmem_limit_bytes=40 << 20),
        cost_estimate=pl.CostEstimate(flops=4 * rows * work, bytes_accessed=8 * nfield * depth * size * xrows,
                                      transcendentals=work),
        name="stencil_chunk",
    )(*operands)


def ring(sizes, offsets):
    pairs = []
    for i in range(sizes[0]):
        for j in range(sizes[1]):
            pairs.append((i * sizes[1] + j, (i + offsets[0]) % sizes[0] * sizes[1] + (j + offsets[1]) % sizes[1]))
    return pairs


def halos(fields_t, edges, halo):
    sizes = (lax.axis_size("sim"), lax.axis_size(("grp", "gz")))
    nfield, depth, ycols, xrows = fields_t.shape

    def send(part, over_x, over_y):
        return lax.ppermute(part, AXES, ring(sizes, (over_x, over_y)))

    if sizes[0] == 2:
        edges = send(edges, 1, 0)
    else:
        edges = jnp.concatenate([send(edges[:, :LANES], -1, 0), send(edges[:, LANES:], 1, 0)], 1)
    joined = -(-2 * LANES // xrows)

    def rows(first, over_y):
        corner = edges[first:first + halo]
        corner = jnp.pad(corner, ((0, 0), (0, joined * xrows - 2 * LANES)))
        corner = jnp.transpose(corner.reshape(halo, joined, xrows), (1, 0, 2))
        part = fields_t[:, :, first:first + halo].reshape(nfield * depth, halo, xrows)
        return send(jnp.concatenate([part, corner], 0), 0, over_y)

    return edges, rows(ycols - halo, 1), rows(0, -1)


def gram_messages(gathered, basis_cols, place):
    n_core, n_grp, n_pair, nf, ycols, rank = gathered.shape
    count = n_core * n_grp * n_pair * ycols
    half = count // 2
    ncols = basis_cols.shape[0] // n_pair
    wide = nf * rank

    def kernel(place_ref, q_ref, by_ref, out_ref, hi, lo, res):
        s, z, x, c = (place_ref[i] for i in range(4))
        for zz in range(n_grp):
            for xx in range(n_pair):
                for cc in range(n_core):
                    row = ((zz * n_pair + xx) * n_core + cc) * ycols
                    for f in range(nf):
                        q = q_ref[cc ^ c, zz ^ z, xx, f]
                        big = q.astype(jnp.bfloat16)
                        hi[row:row + ycols, f * rank:(f + 1) * rank] = big
                        lo[row:row + ycols, f * rank:(f + 1) * rank] = (q - big.astype(jnp.float32)).astype(jnp.bfloat16)
        dims = (((1,), (1,)), ((), ()))
        for dx in range(n_pair):
            row = pl.multiple_of(((z * n_pair + (x ^ dx)) * n_core + c) * ycols, ycols)
            mine_hi = hi[pl.ds(row, ycols), :]
            mine_lo = lo[pl.ds(row, ycols), :]
            for side in range(2):
                cols = slice(side * half, (side + 1) * half)
                part = lax.dot_general(mine_hi, hi[cols, :], dims, preferred_element_type=jnp.float32)
                part += lax.dot_general(mine_lo, hi[cols, :], dims, preferred_element_type=jnp.float32)
                part += lax.dot_general(mine_hi, lo[cols, :], dims, preferred_element_type=jnp.float32)
                out_ref[dx, side ^ s, 0:ycols, :] = part
        core = jnp.dot(by_ref[...], hi[...], preferred_element_type=jnp.float32)
        core += jnp.dot(by_ref[...], lo[...], preferred_element_type=jnp.float32)
        res[...] = core
        keep = rank // 2
        for dx in range(n_pair):
            mine = res[pl.ds(pl.multiple_of((x ^ dx) * ncols, ncols), ncols), :]
            for side in range(2):
                parts = [mine[:, f * rank + side * keep:f * rank + (side + 1) * keep] for f in range(nf)]
                parts.append(jnp.zeros((ncols, half - nf * keep), jnp.float32))
                out_ref[dx, side ^ s, ycols:ycols + ncols, :] = jnp.concatenate(parts, 1)

    return pl.pallas_call(
        kernel,
        in_specs=[pl.BlockSpec(memory_space=pltpu.SMEM)] + [pl.BlockSpec(memory_space=pltpu.VMEM)] * 2,
        out_shape=jax.ShapeDtypeStruct((n_pair, 2, ycols + ncols, half), jnp.float32),
        scratch_shapes=[pltpu.VMEM((count, wide), jnp.bfloat16)] * 2 + [pltpu.VMEM((n_pair * ncols, wide), jnp.float32)],
        compiler_params=pltpu.CompilerParams(vmem_limit_bytes=32 << 20),
        cost_estimate=pl.CostEstimate(flops=6 * 2 * ycols * count * wide, bytes_accessed=8 * count * wide, transcendentals=0),
        name="gram_messages",
    )(place, gathered, basis_cols)


def finish_y(pieces, place, nf, ycols, scale):
    rows, half = pieces[0].shape
    ncols = rows - ycols

    def kernel(place_ref, a_ref, b_ref, c_ref, d_ref, gram_ref, core_ref):
        s, x = place_ref[0], place_ref[2]
        refs = (a_ref, b_ref, c_ref, d_ref)
        gram_ref[...] = ((a_ref[0:ycols, :] + b_ref[0:ycols, :]) + (c_ref[0:ycols, :] + d_ref[0:ycols, :])) * scale
        r = core_ref.shape[3]
        for dx in range(2):
            for ds in range(2):
                piece = refs[2 * dx + ds][ycols:rows, :]
                for f in range(nf):
                    core_ref[(x ^ dx) * nf + f, s ^ ds] = piece[:, f * r:(f + 1) * r]

    def call(r):
        return pl.pallas_call(
            kernel,
            in_specs=[pl.BlockSpec(memory_space=pltpu.SMEM)] + [pl.BlockSpec(memory_space=pltpu.VMEM)] * 4,
            out_shape=(jax.ShapeDtypeStruct((ycols, half), jnp.float32),
                       jax.ShapeDtypeStruct((2 * nf, 2, ncols, r), jnp.float32)),
            name="finish_y",
        )(place, *pieces)

    return call


def pairwise(state_t, mine, theirs, basis_x, basis_y):
    n_grp, n_gz = lax.axis_size("grp"), lax.axis_size("gz")
    nfield, depth, ycols, xrows = state_t.shape
    rank = basis_x.shape[1]
    size = 2 * n_grp * n_gz
    core_bit, pair_bit, near_bit, far_bit, sim_bit = 1, n_gz // 2, n_gz, 2 * n_gz, n_grp * n_gz
    s, z, gz = lax.axis_index("sim"), lax.axis_index("grp"), lax.axis_index("gz")
    x, c = gz // 2, gz % 2
    place = jnp.stack([s, z, x, c]).astype(jnp.int32)

    def swap(part, bits, name):
        with jax.named_scope(name):
            return lax.ppermute(part, AXES, [(i, i ^ bits) for i in range(size)])

    def pick(part, index, axis):
        return lax.dynamic_index_in_dim(part, index, axis, keepdims=False)

    def project(part, side):
        rows = lax.dynamic_slice_in_dim(basis_x, side * xrows, xrows, 0).astype(jnp.float32)
        return jnp.einsum("fyx,xr->fyr", part, rows, precision=high)

    proj = project(mine, s) + project(theirs, 1 - s)
    proj = proj.reshape(2, nfield // 2, ycols, rank)
    own, got = pick(proj, x, 0), swap(pick(proj, 1 - x, 0), pair_bit, "q_pair")
    pair = jnp.where(x == 0, jnp.stack([own, got]), jnp.stack([got, own]))
    far = swap(pair, far_bit, "q_far")
    near = swap(pair, near_bit, "q_near")
    both = swap(far, near_bit, "q_both")
    chip = jnp.stack([pair, near, far, both])
    gathered = jnp.stack([chip, swap(chip, core_bit, "q_core")])
    by = basis_y.T.reshape(n_grp, 2, 2, rank // (n_grp * n_gz), -1)
    by = pick(pick(by, c, 2), z, 0).reshape(-1, basis_y.shape[0])
    messages = gram_messages(gathered, by, place)
    pieces = [messages[0, 0], swap(messages[0, 1], sim_bit, "y_sim"), swap(messages[1, 0], pair_bit, "y_pair"),
              swap(messages[1, 1], sim_bit | pair_bit, "y_diag")]
    gram_y, core = finish_y(pieces, place, nfield // 2, ycols, 1.0 / (nfield * depth * rank))(rank // 2)

    def fold(block, name):
        block = block.reshape(-1, 2, 2, 2, ycols, xrows)
        block = pick(block, c, 3) + swap(pick(block, 1 - c, 3), core_bit, name + "_core")
        return pick(block, x, 2) + swap(pick(block, 1 - x, 2), pair_bit, name + "_pair")

    same = fold(jnp.einsum("fzyw,fzyx->wx", state_t, state_t, precision=high), "same")[0]
    cross = jnp.einsum("fyw,fyx->wx", theirs, mine, precision=high)
    cross = fold(jnp.stack([cross, cross.T]), "cross")
    cross = cross[0] + swap(cross[1], sim_bit, "cross_sim")
    at_home = z // 2 == s
    kept = jnp.where(at_home, same, cross) + swap(jnp.where(at_home, cross, same), far_bit, "x_far")
    gram_x = pick(kept, z % 2, 0) + swap(pick(kept, 1 - z % 2, 0), near_bit, "x_near")
    gram_x = gram_x * (1.0 / (nfield * depth * ycols * n_grp * n_gz))
    return gram_x.T, gram_y, jnp.transpose(core, (0, 1, 3, 2))


def collective(state, basis_x, basis_y):
    nfield, depth, x_rows, ycols = state.shape
    rank = basis_y.shape[1]
    n_y = lax.axis_size(("grp", "gz"))
    basis_xf = basis_x.astype(jnp.float32)
    basis_yf = basis_y.astype(jnp.float32)
    gram_rows = jnp.einsum(
        "fzxy,fzwy->xw", state, lax.all_gather(state, "sim", axis=2, tiled=True), precision=highest
    )
    own_basis = lax.dynamic_slice_in_dim(basis_xf, lax.axis_index("sim") * x_rows, x_rows, 0)
    partial_proj = jnp.einsum("xr,fzxy->fzry", own_basis, state, precision=highest)
    projected = lax.psum_scatter(partial_proj, "sim", scatter_dimension=2, tiled=True)
    gram_x = lax.psum_scatter(gram_rows, ("grp", "gz"), scatter_dimension=1, tiled=True) / (
        nfield * depth * ycols * n_y
    )
    rank_grp = rank // n_y
    rank_cols_y = lax.dynamic_slice_in_dim(basis_yf, lax.axis_index(("grp", "gz")) * rank_grp, rank_grp, 1)
    incoming = lax.all_gather(projected, ("grp", "gz"), axis=3, tiled=True)
    block = jnp.einsum("fzry,fzrv->yv", projected, incoming, precision=highest)
    core_part = jnp.einsum("vs,fzrv->fzrs", rank_cols_y, incoming, precision=highest)
    gram_y = lax.psum_scatter(block, "sim", scatter_dimension=1, tiled=True) / (nfield * depth * rank)
    return gram_x, gram_y, core_part


def shards(fields, diffusivity, velocity, coupling, basis_x, basis_y):
    halo = STAGES * STEPS
    fields_t = jnp.transpose(fields, (0, 1, 3, 2))
    nfield, depth, ycols, _ = fields_t.shape
    sizes = tuple(lax.axis_size(a) for a in AXES)
    paired = sizes[0] == depth == 2 and sizes[1] == sizes[2] == 4
    side = jnp.reshape(lax.axis_index("sim"), (1,)).astype(jnp.int32)
    span = LANES // (depth * nfield)
    edges, coef, mix = setup(fields_t, diffusivity, velocity, coupling, halo, span)
    edges, above, below = halos(fields_t, edges, halo)
    blocks = [(above, None, None, None)]
    blocks += [(fields_t, i, edges, i * halo) for i in range(ycols // halo)]
    blocks += [(below, None, None, None)]
    size = 2 * halo
    count = ycols // size
    cuts = [0] + [2 + size * (j + 1) // halo for j in range(count)]
    carry = state_t = None
    mine, theirs = [], []
    for j in range(count):
        out = stencil_chunk(fields_t, blocks[cuts[j]:cuts[j + 1]], carry, state_t, coef, mix, side, halo, span, j, size,
                            j == count - 1)
        state_t, give, keep = out[:3]
        carry = out[3] if j < count - 1 else None
        if paired:
            with jax.named_scope("exchange"):
                theirs.append(lax.ppermute(give, "sim", [(0, 1), (1, 0)]))
            mine.append(keep)
    state = jnp.transpose(state_t, (0, 1, 3, 2))
    if paired:
        statistics = pairwise(state_t, jnp.concatenate(mine, 1), jnp.concatenate(theirs, 1), basis_x, basis_y)
    else:
        statistics = collective(state, basis_x, basis_y)
    return (state, *statistics)


def solution(mesh):
    in_specs = (P(None, None, "sim", ("grp", "gz")), P(), P(), P(), P(), P())
    out_specs = (
        P(None, None, "sim", ("grp", "gz")),
        P("sim", ("grp", "gz")),
        P(("grp", "gz"), "sim"),
        P(None, None, "sim", ("grp", "gz")),
    )
    return jax.shard_map(shards, mesh=mesh, in_specs=in_specs, out_specs=out_specs, check_vma=False)
```

```python
import jax
import jax.numpy as jnp
from jax import lax
from jax.experimental import pallas as pl
from jax.experimental.pallas import tpu as pltpu
from jax.sharding import PartitionSpec as P


STEPS = 2
BANDS = 4
STAGES = 4
LANES = 128
AXES = ("sim", "grp", "gz")
time_step = 1.0
high = lax.Precision.HIGH
highest = lax.Precision.HIGHEST


def setup(fields_t, diffusivity, velocity, coupling, halo, span):
    nfield, depth, ycols, xrows = fields_t.shape
    width = min(xrows, LANES)
    rows = depth * span * nfield
    half = 0.5 * time_step

    def kernel(first_ref, last_ref, d_ref, v_ref, c_ref, edge_ref, coef_ref, mix_ref):
        lane = lax.broadcasted_iota(jnp.int32, (ycols, LANES), 1)
        head = jnp.zeros((ycols, LANES), jnp.float32)
        tail = jnp.zeros((ycols, LANES), jnp.float32)
        for z in range(depth):
            for f in range(nfield):
                at = (z * nfield + f) * halo
                left, right = first_ref[f, z], last_ref[f, z]
                if width < LANES:
                    fill = jnp.zeros((ycols, LANES - width), jnp.float32)
                    left, right = jnp.concatenate([left, fill], 1), jnp.concatenate([right, fill], 1)
                mine = (lane >= at) & (lane < at + halo)
                head = jnp.where(mine, pltpu.roll(left, at, 1) if at else left, head)
                shift = (at - (width - halo)) % LANES
                tail = jnp.where(mine, pltpu.roll(right, shift, 1) if shift else right, tail)
        edge_ref[:, 0:LANES] = head
        edge_ref[:, LANES:2 * LANES] = tail
        sub = lax.broadcasted_iota(jnp.int32, (nfield, LANES), 0)

        def column(values):
            out = jnp.zeros((nfield, LANES), jnp.float32)
            for f in range(nfield):
                out = jnp.where(sub == f, values[f], out)
            return out

        d = column([d_ref[f] for f in range(nfield)]) * half
        vx = column([v_ref[0, f] for f in range(nfield)]) * (0.5 * half)
        vy = column([v_ref[1, f] for f in range(nfield)]) * (0.5 * half)
        for i, value in enumerate((-6.0 * d, 2.0 * d, d - vy, d + vy, d - vx, d + vx)):
            coef_ref[i] = value
        sub = lax.broadcasted_iota(jnp.int32, (nfield, rows), 0)
        mod = lax.broadcasted_iota(jnp.int32, (nfield, rows), 1) % nfield
        block = lax.broadcasted_iota(jnp.int32, (nfield, rows), 1) // nfield
        tile = jnp.zeros((nfield, rows), jnp.float32)
        for g in range(nfield):
            value = jnp.zeros((nfield, rows), jnp.float32)
            for f in range(nfield):
                value = jnp.where(sub == f, c_ref[f, g] * half, value)
            tile = jnp.where(mod == g, value, tile)
        hi = tile.astype(jnp.bfloat16).astype(jnp.float32)
        lo = tile - hi
        for part, base in ((hi, 0), (lo, rows)):
            for i in range(0, rows // nfield, 2):
                value = jnp.concatenate([jnp.where(block == i + k, part, 0.0) for k in range(2)], 0).astype(jnp.bfloat16)
                for j in range(2):
                    mix_ref[base + i * nfield:base + (i + 2) * nfield, j * rows:(j + 1) * rows] = value

    smem = pl.BlockSpec(memory_space=pltpu.SMEM)
    last = xrows // width - 1
    return pl.pallas_call(
        kernel,
        grid=(1,),
        in_specs=[pl.BlockSpec((nfield, depth, ycols, width), lambda i: (0, 0, 0, 0)),
                  pl.BlockSpec((nfield, depth, ycols, width), lambda i: (0, 0, 0, last)), smem, smem, smem],
        out_shape=(jax.ShapeDtypeStruct((ycols, 2 * LANES), jnp.float32),
                   jax.ShapeDtypeStruct((6, nfield, LANES), jnp.float32),
                   jax.ShapeDtypeStruct((2 * rows, 2 * rows), jnp.bfloat16)),
        out_specs=(pl.BlockSpec((ycols, 2 * LANES), lambda i: (0, 0)),
                   pl.BlockSpec((6, nfield, LANES), lambda i: (0, 0, 0)),
                   pl.BlockSpec((2 * rows, 2 * rows), lambda i: (0, 0))),
        name="setup",
    )(fields_t, fields_t, diffusivity, velocity, coupling)


def stencil_chunk(fields_t, blocks, carry, filled, coef, mix, side, halo, span, index, size, final):
    nfield, depth, _, xrows = fields_t.shape
    lanes = -(-(xrows + 2 * halo) // LANES) * LANES
    tiles = lanes // LANES
    whole = xrows // LANES
    rows = depth * span * nfield
    stages = STEPS * STAGES
    keep = halo + 1
    old = 0 if carry is None else keep
    win = old + halo * len(blocks)
    start = xrows - whole * LANES
    n = len(blocks)
    u, p, q, acc = range(4)
    joined_rows = -(-2 * LANES // xrows)

    def kernel(*refs):
        side_ref, refs = refs[0], refs[1:]
        sources, refs = refs[:n], refs[n:]
        edges = [None if b[2] is None else refs[0] for b in blocks]
        refs = refs[1:]
        carry_ref = None
        if carry is not None:
            carry_ref, refs = refs[0], refs[2:]
        coef_ref, mix_ref, out_ref, give_ref, mine_ref = refs[:5]
        refs = refs[5:]
        left_ref = None
        if not final:
            left_ref, refs = refs[0], refs[1:]
        bufs, tcat, react = refs
        lane = lax.broadcasted_iota(jnp.int32, (halo, LANES), 1)
        column = lax.broadcasted_iota(jnp.int32, (nfield, LANES), 1)
        is_last = column == LANES - 1
        is_first = column == 0

        def place(z, row, count=1):
            return pl.ds(pl.multiple_of((z * win + row) * nfield, nfield), count * nfield)

        def strided(z, row, f, count):
            return pl.ds((z * win + row) * nfield + f, count, stride=nfield)

        def edge_of(i):
            if blocks[i][2] is None:
                parts = [sources[i][nfield * depth + k] for k in range(joined_rows)]
                both = parts[0] if joined_rows == 1 else jnp.concatenate(parts, 1)
            else:
                both = edges[i][blocks[i][3]:blocks[i][3] + halo, :]
            return both[:, 0:LANES], both[:, LANES:2 * LANES]

        for z in range(depth):
            if carry is not None:
                for b in range(4):
                    for tile in range(tiles):
                        bufs[b, tile, place(z, 0, keep), :] = carry_ref[b, tile, z]
            else:
                for b in (p, q):
                    for tile in range(tiles):
                        bufs[b, tile, place(z, 0), :] = jnp.zeros((nfield, LANES), jnp.float32)
            if final:
                for b in (p, q):
                    for tile in range(tiles):
                        bufs[b, tile, place(z, win - 1), :] = jnp.zeros((nfield, LANES), jnp.float32)
            for f in range(nfield):
                at = (z * nfield + f) * halo
                for i in range(n):
                    row = old + i * halo
                    whose = (f, z) if blocks[i][2] is not None else (f * depth + z,)
                    for tile in range(whole):
                        bufs[u, tile, strided(z, row, f, halo), :] = sources[i][(*whose, slice(None), slice(tile * LANES, (tile + 1) * LANES))]
                    after, before = edge_of(i)
                    sa, sb = (start - at) % LANES, (LANES - halo - at) % LANES
                    after = pltpu.roll(after, sa, 1) if sa else after
                    before = pltpu.roll(before, sb, 1) if sb else before
                    base = jnp.zeros((halo, LANES), jnp.float32)
                    if start:
                        part = sources[i][(*whose, slice(None), slice(whole * LANES, xrows))]
                        base = jnp.concatenate([part, jnp.zeros((halo, LANES - start), jnp.float32)], 1)
                    value = jnp.where((lane >= start) & (lane < start + halo), after, base)
                    bufs[u, tiles - 1, strided(z, row, f, halo), :] = jnp.where(lane >= LANES - halo, before, value)

        def prepare(src, row, slot):
            for z in range(depth):
                for r in range(0, span, 2):
                    for tile in range(tiles):
                        t = jnp.tanh(bufs[src, tile, place(z, row + r, 2), :])
                        hi = t.astype(jnp.bfloat16)
                        lo = (t - hi.astype(jnp.float32)).astype(jnp.bfloat16)
                        k = (z * span + r) * nfield
                        cols = slice(tile * LANES, (tile + 1) * LANES)
                        tcat[slot, k:k + 2 * nfield, cols] = hi
                        tcat[slot, rows + k:rows + k + 2 * nfield, cols] = lo

        def extent(k):
            low = keep - k if carry is not None else k
            top = win - k
            return top, (top - low + span - 1) // span

        def first_row(k):
            top, count = extent(k)
            return jnp.maximum(top - span * count, 1)

        def stage(which, k, slot):
            src, dst = (u, p, q, p)[which], (p, q, p, u)[which]
            c = [coef_ref[i] for i in range(6)]
            top, count = extent(k)
            following = first_row(jnp.minimum(k + 1, stages))

            def body(g, slot):
                row = jnp.maximum(top - span * (count - g), 1)
                ends = g == count - 1
                nxt = jnp.where(ends, following, jnp.maximum(top - span * (count - g - 1), 1))
                both = jnp.dot(mix_ref[...], tcat[slot], preferred_element_type=jnp.float32)
                react[...] = both[:rows] + both[rows:]
                for z in range(depth):
                    for r in range(span):
                        k = (z * span + r) * nfield
                        here = place(z, row + r)
                        mids = [bufs[src, tile, here, :] for tile in range(tiles)]
                        ups = [pltpu.roll(m, LANES - 1, 1) for m in mids]
                        downs = [pltpu.roll(m, 1, 1) for m in mids]
                        for tile in range(tiles):
                            mid = mids[tile]

                            def near(zz, rr):
                                return bufs[src, tile, place(zz % depth, row + rr), :]

                            h = react[k:k + nfield, tile * LANES:(tile + 1) * LANES] + c[0] * mid
                            if depth == 2:
                                h = h + c[1] * near(1 - z, r)
                            else:
                                h = h + (0.5 * c[1]) * (near(z + 1, r) + near(z - 1, r))
                            h = h + c[2] * near(z, r + 1) + c[3] * near(z, r - 1)
                            h = h + c[4] * jnp.where(is_last, ups[(tile + 1) % tiles], ups[tile])
                            h = h + c[5] * jnp.where(is_first, downs[(tile - 1) % tiles], downs[tile])
                            if which == 0:
                                bufs[dst, tile, here, :] = mid + h
                            elif which == 1:
                                y = bufs[u, tile, here, :] + h
                                bufs[dst, tile, here, :] = y
                                bufs[acc, tile, here, :] = mid + y + h
                            elif which == 2:
                                bufs[dst, tile, here, :] = bufs[u, tile, here, :] + (h + h)
                            else:
                                bufs[dst, tile, here, :] = (bufs[acc, tile, here, :] + mid + h) * (1.0 / 3.0)
                prepare(jnp.where(ends, dst, src), nxt, 1 - slot)
                return 1 - slot

            return lax.fori_loop(0, count, body, slot)

        prepare(u, first_row(1), 0)

        def step(i, slot):
            for which in range(STAGES):
                slot = stage(which, i * STAGES + which + 1, slot)
            return slot

        lax.fori_loop(0, STEPS, step, 0)
        bottom = win - halo - size
        s = side_ref[0]
        for f in range(nfield):
            for tile in range(whole + (start > 0)):
                width = LANES if tile < whole else start
                cols = slice(tile * LANES, tile * LANES + width)
                for z in range(depth):
                    out_ref[f, z, :, cols] = bufs[u, tile, strided(z, bottom, f, size), :][:, :width]
                give_ref[f, :, cols] = bufs[u, tile, strided((s + 1) % depth, bottom, f, size), :][:, :width]
                mine_ref[f, :, cols] = bufs[u, tile, strided(s % depth, bottom, f, size), :][:, :width]
        if not final:
            for z in range(depth):
                for b in range(4):
                    for tile in range(tiles):
                        left_ref[b, tile, z] = bufs[b, tile, place(z, win - keep, keep), :]

    vmem = pl.BlockSpec(memory_space=pltpu.VMEM)
    specs = [pl.BlockSpec(memory_space=pltpu.SMEM)]
    for array, at, edge, _ in blocks:
        if edge is None:
            specs.append(vmem)
        else:
            specs.append(pl.BlockSpec((nfield, depth, halo, xrows), (lambda i, at=at: (0, 0, at, 0))))
    specs.append(vmem)
    operands = [side, *(b[0] for b in blocks), next(b[2] for b in blocks if b[2] is not None)]
    aliases = {}
    if carry is not None:
        operands += [carry, filled]
        specs += [vmem, pl.BlockSpec(memory_space=pl.ANY)]
        aliases = {len(operands) - 1: 0}
    operands += [coef, mix]
    specs += [vmem, vmem]
    part = jax.ShapeDtypeStruct((nfield, size, xrows), jnp.float32)
    part_spec = pl.BlockSpec((nfield, size, xrows), lambda i: (0, 0, 0))
    shapes = [jax.ShapeDtypeStruct(fields_t.shape, jnp.float32), part, part]
    out_specs = [pl.BlockSpec((nfield, depth, size, xrows), lambda i: (0, 0, index, 0)), part_spec, part_spec]
    if not final:
        left = (4, tiles, depth, keep * nfield, LANES)
        shapes.append(jax.ShapeDtypeStruct(left, jnp.float32))
        out_specs.append(pl.BlockSpec(left, lambda i: (0, 0, 0, 0, 0)))
    work = sum(-(-(win - old - (0 if old else 2 * k)) // span) for k in range(1, stages + 1)) * rows * lanes
    return pl.pallas_call(
        kernel,
        grid=(1,),
        in_specs=specs,
        out_specs=out_specs,
        out_shape=shapes,
        scratch_shapes=[pltpu.VMEM((4, tiles, depth * win * nfield, LANES), jnp.float32),
                        pltpu.VMEM((2, 2 * rows, lanes), jnp.bfloat16),
                        pltpu.VMEM((rows, lanes), jnp.float32)],
        input_output_aliases=aliases,
        compiler_params=pltpu.CompilerParams(vmem_limit_bytes=40 << 20),
        cost_estimate=pl.CostEstimate(flops=4 * rows * work, bytes_accessed=8 * nfield * depth * size * xrows,
                                      transcendentals=work),
        name="stencil_chunk",
    )(*operands)


def ring(sizes, offsets):
    pairs = []
    for i in range(sizes[0]):
        for j in range(sizes[1]):
            pairs.append((i * sizes[1] + j, (i + offsets[0]) % sizes[0] * sizes[1] + (j + offsets[1]) % sizes[1]))
    return pairs


def halos(fields_t, edges, halo):
    sizes = (lax.axis_size("sim"), lax.axis_size(("grp", "gz")))
    nfield, depth, ycols, xrows = fields_t.shape

    def send(part, over_x, over_y):
        return lax.ppermute(part, AXES, ring(sizes, (over_x, over_y)))

    if sizes[0] == 2:
        edges = send(edges, 1, 0)
    else:
        edges = jnp.concatenate([send(edges[:, :LANES], -1, 0), send(edges[:, LANES:], 1, 0)], 1)
    joined = -(-2 * LANES // xrows)

    def rows(first, over_y):
        corner = edges[first:first + halo]
        corner = jnp.pad(corner, ((0, 0), (0, joined * xrows - 2 * LANES)))
        corner = jnp.transpose(corner.reshape(halo, joined, xrows), (1, 0, 2))
        part = fields_t[:, :, first:first + halo].reshape(nfield * depth, halo, xrows)
        return send(jnp.concatenate([part, corner], 0), 0, over_y)

    return edges, rows(ycols - halo, 1), rows(0, -1)


def gram_messages(gathered, basis_cols, place):
    n_core, n_grp = len(gathered), len(gathered[0])
    n_pair, nf, ycols, rank = gathered[0][0].shape
    count = n_core * n_grp * n_pair * ycols
    half = count // 2
    ncols = basis_cols.shape[0] // n_pair
    wide = nf * rank

    def kernel(place_ref, by_ref, *refs):
        q_refs, refs = refs[:n_core * n_grp], refs[n_core * n_grp:]
        outs, (hi, lo, res) = refs[:2 * n_pair], refs[2 * n_pair:]
        s, z, x, c = (place_ref[i] for i in range(4))
        for dz in range(n_grp):
            for xx in range(n_pair):
                for dc in range(n_core):
                    row = pl.multiple_of((((z ^ dz) * n_pair + xx) * n_core + (c ^ dc)) * ycols, ycols)
                    for f in range(nf):
                        q = q_refs[dc * n_grp + dz][xx, f]
                        big = q.astype(jnp.bfloat16)
                        hi[pl.ds(row, ycols), f * rank:(f + 1) * rank] = big
                        lo[pl.ds(row, ycols), f * rank:(f + 1) * rank] = (q - big.astype(jnp.float32)).astype(jnp.bfloat16)
        dims = (((1,), (1,)), ((), ()))
        for dx in range(n_pair):
            row = pl.multiple_of(((z * n_pair + (x ^ dx)) * n_core + c) * ycols, ycols)
            mine_hi = hi[pl.ds(row, ycols), :]
            mine_lo = lo[pl.ds(row, ycols), :]
            for ds in range(2):
                cols = pl.ds(pl.multiple_of((s ^ ds) * half, half), half)
                part = lax.dot_general(mine_hi, hi[cols, :], dims, preferred_element_type=jnp.float32)
                part += lax.dot_general(mine_lo, hi[cols, :], dims, preferred_element_type=jnp.float32)
                part += lax.dot_general(mine_hi, lo[cols, :], dims, preferred_element_type=jnp.float32)
                outs[2 * dx + ds][0:ycols, :] = part
        core = jnp.dot(by_ref[...], hi[...], preferred_element_type=jnp.float32)
        core += jnp.dot(by_ref[...], lo[...], preferred_element_type=jnp.float32)
        res[...] = core
        keep = rank // 2
        for dx in range(n_pair):
            mine = res[pl.ds(pl.multiple_of((x ^ dx) * ncols, ncols), ncols), :]
            packs = []
            for side in range(2):
                parts = [mine[:, f * rank + side * keep:f * rank + (side + 1) * keep] for f in range(nf)]
                parts.append(jnp.zeros((ncols, half - nf * keep), jnp.float32))
                packs.append(jnp.concatenate(parts, 1))
            for ds in range(2):
                outs[2 * dx + ds][ycols:ycols + ncols, :] = jnp.where((s ^ ds) == 0, packs[0], packs[1])

    return pl.pallas_call(
        kernel,
        in_specs=[pl.BlockSpec(memory_space=pltpu.SMEM)] + [pl.BlockSpec(memory_space=pltpu.VMEM)] * (1 + n_core * n_grp),
        out_shape=[jax.ShapeDtypeStruct((ycols + ncols, half), jnp.float32)] * (2 * n_pair),
        scratch_shapes=[pltpu.VMEM((count, wide), jnp.bfloat16)] * 2 + [pltpu.VMEM((n_pair * ncols, wide), jnp.float32)],
        compiler_params=pltpu.CompilerParams(vmem_limit_bytes=32 << 20),
        cost_estimate=pl.CostEstimate(flops=6 * 2 * ycols * count * wide, bytes_accessed=8 * count * wide, transcendentals=0),
        name="gram_messages",
    )(place, basis_cols, *(part for side in gathered for part in side))


def finish_y(pieces, place, nf, ycols, scale):
    rows, half = pieces[0].shape
    ncols = rows - ycols

    def kernel(place_ref, a_ref, b_ref, c_ref, d_ref, gram_ref, core_ref):
        s, x = place_ref[0], place_ref[2]
        refs = (a_ref, b_ref, c_ref, d_ref)
        gram_ref[...] = ((a_ref[0:ycols, :] + b_ref[0:ycols, :]) + (c_ref[0:ycols, :] + d_ref[0:ycols, :])) * scale
        r = core_ref.shape[3]
        for dx in range(2):
            for ds in range(2):
                piece = refs[2 * dx + ds][ycols:rows, :]
                for f in range(nf):
                    core_ref[(x ^ dx) * nf + f, s ^ ds] = piece[:, f * r:(f + 1) * r]

    def call(r):
        return pl.pallas_call(
            kernel,
            in_specs=[pl.BlockSpec(memory_space=pltpu.SMEM)] + [pl.BlockSpec(memory_space=pltpu.VMEM)] * 4,
            out_shape=(jax.ShapeDtypeStruct((ycols, half), jnp.float32),
                       jax.ShapeDtypeStruct((2 * nf, 2, ncols, r), jnp.float32)),
            name="finish_y",
        )(place, *pieces)

    return call


def after(value, *first):
    return lax.optimization_barrier((value, *first))[0]


def pairwise(state_t, mine, theirs, basis_x, basis_y):
    n_grp, n_gz = lax.axis_size("grp"), lax.axis_size("gz")
    nfield, depth, ycols, xrows = state_t.shape
    rank = basis_x.shape[1]
    size = 2 * n_grp * n_gz
    core_bit, pair_bit, near_bit, far_bit, sim_bit = 1, n_gz // 2, n_gz, 2 * n_gz, n_grp * n_gz
    s, z, gz = lax.axis_index("sim"), lax.axis_index("grp"), lax.axis_index("gz")
    x, c = gz // 2, gz % 2
    place = jnp.stack([s, z, x, c]).astype(jnp.int32)

    def swap(part, bits):
        return lax.ppermute(part, AXES, [(i, i ^ bits) for i in range(size)])

    def pick(part, index, axis):
        return lax.dynamic_index_in_dim(part, index, axis, keepdims=False)

    own_rows = lax.dynamic_slice_in_dim(basis_x, s * xrows, xrows, 0).astype(jnp.float32)
    their_rows = lax.dynamic_slice_in_dim(basis_x, (1 - s) * xrows, xrows, 0).astype(jnp.float32)
    by = basis_y.T.reshape(n_grp, 2, 2, rank // (n_grp * n_gz), -1)
    by = pick(pick(by, c, 2), z, 0).reshape(-1, basis_y.shape[0])

    same = jnp.einsum("fzyw,fzyx->wx", state_t, state_t, precision=high).reshape(2, 2, 2, ycols, xrows)
    same_send = pick(same, 1 - c, 2)
    same_got = swap(same_send, core_bit)

    proj = jnp.einsum("fyx,xr->fyr", mine, own_rows, precision=high) + jnp.einsum(
        "fyx,xr->fyr", theirs, their_rows, precision=high)
    proj = proj.reshape(2, nfield // 2, ycols, rank)
    q_send = pick(proj, 1 - x, 0)
    q_got = swap(q_send, pair_bit)

    cross = jnp.einsum("fyw,fyx->wx", after(theirs, q_send), mine, precision=high)
    cross = jnp.stack([cross, cross.T]).reshape(2, 2, 2, 2, ycols, xrows)
    cross_send = pick(cross, 1 - c, 3)
    cross_got = swap(cross_send, core_bit)

    same = pick(same, c, 2) + same_got
    same_send = pick(same, 1 - x, 1)
    same_got = swap(same_send, pair_bit)

    own = pick(proj, x, 0)
    pair = jnp.where(x == 0, jnp.stack([own, q_got]), jnp.stack([q_got, own]))
    far = swap(pair, far_bit)
    near = swap(pair, near_bit)

    cross = pick(cross, c, 3) + cross_got
    cross_here, cross_there = pick(cross, x, 2), pick(cross, 1 - x, 2)
    got_pair = swap(cross_there[0], pair_bit)
    got_sim = swap(cross_here[1], sim_bit)
    got_diag = swap(cross_there[1], sim_bit | pair_bit)

    both = swap(far, near_bit)
    near_core = swap(near, core_bit)
    pair_core = swap(pair, core_bit)
    far_core = swap(far, core_bit)
    at_home = z // 2 == s
    zero = z % 2
    same = pick(same, x, 1) + same_got
    cross = (cross_here[0] + got_pair) + (got_sim + got_diag)
    kept, passed = jnp.where(at_home, same, cross), jnp.where(at_home, cross, same)
    own_block = pick(kept, zero, 0)
    to_near, to_far, to_both = pick(kept, 1 - zero, 0), pick(passed, zero, 0), pick(passed, 1 - zero, 0)
    x_far = swap(to_far, far_bit)
    x_both = swap(to_both, far_bit | near_bit)
    x_near = swap(to_near, near_bit)

    both_core = swap(both, core_bit)
    gathered = [[pair, near, far, both], [pair_core, near_core, far_core, both_core]]
    messages = gram_messages(gathered, by, place)
    y_diag = swap(messages[3], sim_bit | pair_bit)
    y_pair = swap(messages[2], pair_bit)
    y_sim = swap(messages[1], sim_bit)

    gram_x = (own_block + x_near) + (x_far + x_both)
    gram_x = gram_x * (1.0 / (nfield * depth * ycols * n_grp * n_gz))
    pieces = [messages[0], y_sim, y_pair, y_diag]
    gram_y, core = finish_y(pieces, place, nfield // 2, ycols, 1.0 / (nfield * depth * rank))(rank // 2)
    return gram_x.T, gram_y, jnp.transpose(core, (0, 1, 3, 2))


def collective(state, basis_x, basis_y):
    nfield, depth, x_rows, ycols = state.shape
    rank = basis_y.shape[1]
    n_y = lax.axis_size(("grp", "gz"))
    basis_xf = basis_x.astype(jnp.float32)
    basis_yf = basis_y.astype(jnp.float32)
    gram_rows = jnp.einsum(
        "fzxy,fzwy->xw", state, lax.all_gather(state, "sim", axis=2, tiled=True), precision=highest
    )
    own_basis = lax.dynamic_slice_in_dim(basis_xf, lax.axis_index("sim") * x_rows, x_rows, 0)
    partial_proj = jnp.einsum("xr,fzxy->fzry", own_basis, state, precision=highest)
    projected = lax.psum_scatter(partial_proj, "sim", scatter_dimension=2, tiled=True)
    gram_x = lax.psum_scatter(gram_rows, ("grp", "gz"), scatter_dimension=1, tiled=True) / (
        nfield * depth * ycols * n_y
    )
    rank_grp = rank // n_y
    rank_cols_y = lax.dynamic_slice_in_dim(basis_yf, lax.axis_index(("grp", "gz")) * rank_grp, rank_grp, 1)
    incoming = lax.all_gather(projected, ("grp", "gz"), axis=3, tiled=True)
    block = jnp.einsum("fzry,fzrv->yv", projected, incoming, precision=highest)
    core_part = jnp.einsum("vs,fzrv->fzrs", rank_cols_y, incoming, precision=highest)
    gram_y = lax.psum_scatter(block, "sim", scatter_dimension=1, tiled=True) / (nfield * depth * rank)
    return gram_x, gram_y, core_part


def is_paired(n_sim, n_grp, n_gz):
    return n_sim == 2 and n_grp == n_gz == 4


def compute(fields, diffusivity, velocity, coupling, basis_x, basis_y):
    halo = STAGES * STEPS
    fields_t = jnp.transpose(fields, (0, 1, 3, 2))
    nfield, depth, ycols, _ = fields_t.shape
    sizes = tuple(lax.axis_size(a) for a in AXES)
    paired = is_paired(*sizes) and depth == 2
    side = jnp.reshape(lax.axis_index("sim"), (1,)).astype(jnp.int32)
    span = LANES // (depth * nfield)
    edges, coef, mix = setup(fields_t, diffusivity, velocity, coupling, halo, span)
    edges, above, below = halos(fields_t, edges, halo)
    blocks = [(above, None, None, None)]
    blocks += [(fields_t, i, edges, i * halo) for i in range(ycols // halo)]
    blocks += [(below, None, None, None)]
    count = BANDS
    size = ycols // count
    cuts = [0] + [2 + size * (j + 1) // halo for j in range(count)]
    carry = state_t = None
    mine, theirs = [], []
    for j in range(count):
        out = stencil_chunk(fields_t, blocks[cuts[j]:cuts[j + 1]], carry, state_t, coef, mix, side, halo, span, j,
                            size, j == count - 1)
        state_t, give, keep = out[:3]
        carry = out[3] if j < count - 1 else None
        if paired:
            theirs.append(lax.ppermute(give, "sim", [(0, 1), (1, 0)]))
            mine.append(keep)
    state = jnp.transpose(state_t, (0, 1, 3, 2))
    if paired:
        statistics = pairwise(state_t, jnp.concatenate(mine, 1), jnp.concatenate(theirs, 1), basis_x, basis_y)
    else:
        statistics = collective(state, basis_x, basis_y)
    return (state, *statistics)


def solution(mesh):
    in_specs = (P(None, None, "sim", ("grp", "gz")), P(), P(), P(), P(), P())
    out_specs = (
        P(None, None, "sim", ("grp", "gz")),
        P("sim", ("grp", "gz")),
        P(("grp", "gz"), "sim"),
        P(None, None, "sim", ("grp", "gz")),
    )
    step = jax.shard_map(compute, mesh=mesh, in_specs=in_specs, out_specs=out_specs, check_vma=False)
    if not is_paired(mesh.shape["sim"], mesh.shape["grp"], mesh.shape["gz"]):
        return step
    return step
```

```python
import jax
import jax.numpy as jnp
from jax import lax
from jax.experimental import pallas as pl
from jax.experimental.pallas import tpu as pltpu
from jax.sharding import PartitionSpec as P


STEPS = 2
BANDS = 4
STAGES = 4
LANES = 128
AXES = ("sim", "grp", "gz")
time_step = 1.0
high = lax.Precision.HIGH
highest = lax.Precision.HIGHEST


def x_edges(fields_t, halo):
    nfield, depth, ycols, xrows = fields_t.shape
    width = min(xrows, LANES)

    def kernel(first_ref, last_ref, edge_ref):
        lane = lax.broadcasted_iota(jnp.int32, (ycols, LANES), 1)
        head = jnp.zeros((ycols, LANES), jnp.float32)
        tail = jnp.zeros((ycols, LANES), jnp.float32)
        for z in range(depth):
            for f in range(nfield):
                at = (z * nfield + f) * halo
                left, right = first_ref[f, z], last_ref[f, z]
                if width < LANES:
                    fill = jnp.zeros((ycols, LANES - width), jnp.float32)
                    left, right = jnp.concatenate([left, fill], 1), jnp.concatenate([right, fill], 1)
                mine = (lane >= at) & (lane < at + halo)
                head = jnp.where(mine, pltpu.roll(left, at, 1) if at else left, head)
                shift = (at - (width - halo)) % LANES
                tail = jnp.where(mine, pltpu.roll(right, shift, 1) if shift else right, tail)
        edge_ref[:, 0:LANES] = head
        edge_ref[:, LANES:2 * LANES] = tail

    last = xrows // width - 1
    return pl.pallas_call(
        kernel,
        grid=(1,),
        in_specs=[pl.BlockSpec((nfield, depth, ycols, width), lambda i: (0, 0, 0, 0)),
                  pl.BlockSpec((nfield, depth, ycols, width), lambda i: (0, 0, 0, last))],
        out_shape=jax.ShapeDtypeStruct((ycols, 2 * LANES), jnp.float32),
        out_specs=pl.BlockSpec((ycols, 2 * LANES), lambda i: (0, 0)),
        name="x_edges",
    )(fields_t, fields_t)


def coefficients(diffusivity, velocity, coupling, depth, span):
    nfield = diffusivity.shape[0]
    rows = depth * span * nfield
    half = 0.5 * time_step

    def kernel(d_ref, v_ref, c_ref, coef_ref, mix_ref):
        sub = lax.broadcasted_iota(jnp.int32, (nfield, LANES), 0)

        def column(values):
            out = jnp.zeros((nfield, LANES), jnp.float32)
            for f in range(nfield):
                out = jnp.where(sub == f, values[f], out)
            return out

        d = column([d_ref[f] for f in range(nfield)]) * half
        vx = column([v_ref[0, f] for f in range(nfield)]) * (0.5 * half)
        vy = column([v_ref[1, f] for f in range(nfield)]) * (0.5 * half)
        for i, value in enumerate((-6.0 * d, 2.0 * d, d - vy, d + vy, d - vx, d + vx)):
            coef_ref[i] = value
        sub = lax.broadcasted_iota(jnp.int32, (nfield, rows), 0)
        mod = lax.broadcasted_iota(jnp.int32, (nfield, rows), 1) % nfield
        block = lax.broadcasted_iota(jnp.int32, (nfield, rows), 1) // nfield
        tile = jnp.zeros((nfield, rows), jnp.float32)
        for g in range(nfield):
            value = jnp.zeros((nfield, rows), jnp.float32)
            for f in range(nfield):
                value = jnp.where(sub == f, c_ref[f, g] * half, value)
            tile = jnp.where(mod == g, value, tile)
        hi = tile.astype(jnp.bfloat16).astype(jnp.float32)
        lo = tile - hi
        for part, base in ((hi, 0), (lo, rows)):
            for i in range(0, rows // nfield, 2):
                value = jnp.concatenate([jnp.where(block == i + k, part, 0.0) for k in range(2)], 0).astype(jnp.bfloat16)
                for j in range(2):
                    mix_ref[base + i * nfield:base + (i + 2) * nfield, j * rows:(j + 1) * rows] = value

    smem = pl.BlockSpec(memory_space=pltpu.SMEM)
    return pl.pallas_call(
        kernel,
        in_specs=[smem] * 3,
        out_shape=(jax.ShapeDtypeStruct((6, nfield, LANES), jnp.float32),
                   jax.ShapeDtypeStruct((2 * rows, 2 * rows), jnp.bfloat16)),
        cost_estimate=pl.CostEstimate(flops=4 * rows * rows, bytes_accessed=8 * rows * rows, transcendentals=0),
        name="coefficients",
    )(diffusivity, velocity, coupling)


def stencil_chunk(fields_t, blocks, carry, filled, coef, mix, side, halo, span, index, size, final):
    nfield, depth, ycols, xrows = fields_t.shape
    lanes = -(-(xrows + 2 * halo) // LANES) * LANES
    tiles = lanes // LANES
    whole = xrows // LANES
    rows = depth * span * nfield
    stages = STEPS * STAGES
    keep = halo + 1
    old = 0 if carry is None else keep
    win = old + halo * len(blocks)
    start = xrows - whole * LANES
    n = len(blocks)
    u, p, q, acc = range(4)
    joined_rows = -(-2 * LANES // xrows)

    def kernel(*refs):
        side_ref, refs = refs[0], refs[1:]
        sources, refs = refs[:n], refs[n:]
        edges = [None if b[2] is None else refs[0] for b in blocks]
        refs = refs[1:]
        carry_ref = None
        if carry is not None:
            carry_ref, refs = refs[0], refs[2:]
        coef_ref, mix_ref, out_ref, give_ref, mine_ref = refs[:5]
        refs = refs[5:]
        left_ref = None
        if not final:
            left_ref, refs = refs[0], refs[1:]
        bufs, tcat, react = refs
        lane = lax.broadcasted_iota(jnp.int32, (halo, LANES), 1)
        column = lax.broadcasted_iota(jnp.int32, (nfield, LANES), 1)
        is_last = column == LANES - 1
        is_first = column == 0

        def place(z, row, count=1):
            return pl.ds(pl.multiple_of((z * win + row) * nfield, nfield), count * nfield)

        def strided(z, row, f, count):
            return pl.ds((z * win + row) * nfield + f, count, stride=nfield)

        def edge_of(i):
            if blocks[i][2] is None:
                parts = [sources[i][nfield * depth + k] for k in range(joined_rows)]
                both = parts[0] if joined_rows == 1 else jnp.concatenate(parts, 1)
            else:
                both = edges[i][blocks[i][3]:blocks[i][3] + halo, :]
            return both[:, 0:LANES], both[:, LANES:2 * LANES]

        for z in range(depth):
            if carry is not None:
                for b in range(4):
                    for tile in range(tiles):
                        bufs[b, tile, place(z, 0, keep), :] = carry_ref[b, tile, z]
            else:
                for b in (p, q):
                    for tile in range(tiles):
                        bufs[b, tile, place(z, 0), :] = jnp.zeros((nfield, LANES), jnp.float32)
            if final:
                for b in (p, q):
                    for tile in range(tiles):
                        bufs[b, tile, place(z, win - 1), :] = jnp.zeros((nfield, LANES), jnp.float32)
            for f in range(nfield):
                at = (z * nfield + f) * halo
                for i in range(n):
                    row = old + i * halo
                    whose = (f, z) if blocks[i][2] is not None else (f * depth + z,)
                    for tile in range(whole):
                        bufs[u, tile, strided(z, row, f, halo), :] = sources[i][(*whose, slice(None), slice(tile * LANES, (tile + 1) * LANES))]
                    after, before = edge_of(i)
                    sa, sb = (start - at) % LANES, (LANES - halo - at) % LANES
                    after = pltpu.roll(after, sa, 1) if sa else after
                    before = pltpu.roll(before, sb, 1) if sb else before
                    base = jnp.zeros((halo, LANES), jnp.float32)
                    if start:
                        part = sources[i][(*whose, slice(None), slice(whole * LANES, xrows))]
                        base = jnp.concatenate([part, jnp.zeros((halo, LANES - start), jnp.float32)], 1)
                    value = jnp.where((lane >= start) & (lane < start + halo), after, base)
                    bufs[u, tiles - 1, strided(z, row, f, halo), :] = jnp.where(lane >= LANES - halo, before, value)

        def prepare(src, row):
            for z in range(depth):
                for r in range(span):
                    for tile in range(tiles):
                        t = jnp.tanh(bufs[src, tile, place(z, row + r), :])
                        hi = t.astype(jnp.bfloat16)
                        lo = (t - hi.astype(jnp.float32)).astype(jnp.bfloat16)
                        k = (z * span + r) * nfield
                        cols = slice(tile * LANES, (tile + 1) * LANES)
                        tcat[k:k + nfield, cols] = hi
                        tcat[rows + k:rows + k + nfield, cols] = lo

        def extent(k):
            low = keep - k if carry is not None else k
            top = win - k
            return top, (top - low + span - 1) // span

        def first_row(k):
            top, count = extent(k)
            return jnp.maximum(top - span * count, 1)

        def stage(which, k):
            src, dst = (u, p, q, p)[which], (p, q, p, u)[which]
            c = [coef_ref[i] for i in range(6)]
            top, count = extent(k)
            following = first_row(jnp.minimum(k + 1, stages))

            def body(g, done):
                row = jnp.maximum(top - span * (count - g), 1)
                ends = g == count - 1
                nxt = jnp.where(ends, following, jnp.maximum(top - span * (count - g - 1), 1))
                both = jnp.dot(mix_ref[...], tcat[...], preferred_element_type=jnp.float32)
                react[...] = both[:rows] + both[rows:]
                prepare(jnp.where(ends, dst, src), nxt)
                for z in range(depth):
                    for r in range(span):
                        k = (z * span + r) * nfield
                        here = place(z, row + r)
                        mids = [bufs[src, tile, here, :] for tile in range(tiles)]
                        ups = [pltpu.roll(m, LANES - 1, 1) for m in mids]
                        downs = [pltpu.roll(m, 1, 1) for m in mids]
                        for tile in range(tiles):
                            mid = mids[tile]

                            def near(zz, rr):
                                return bufs[src, tile, place(zz % depth, row + rr), :]

                            h = react[k:k + nfield, tile * LANES:(tile + 1) * LANES] + c[0] * mid
                            if depth == 2:
                                h = h + c[1] * near(1 - z, r)
                            else:
                                h = h + (0.5 * c[1]) * (near(z + 1, r) + near(z - 1, r))
                            h = h + c[2] * near(z, r + 1) + c[3] * near(z, r - 1)
                            h = h + c[4] * jnp.where(is_last, ups[(tile + 1) % tiles], ups[tile])
                            h = h + c[5] * jnp.where(is_first, downs[(tile - 1) % tiles], downs[tile])
                            if which == 0:
                                bufs[dst, tile, here, :] = mid + h
                            elif which == 1:
                                y = bufs[u, tile, here, :] + h
                                bufs[dst, tile, here, :] = y
                                bufs[acc, tile, here, :] = mid + y + h
                            elif which == 2:
                                bufs[dst, tile, here, :] = bufs[u, tile, here, :] + (h + h)
                            else:
                                bufs[dst, tile, here, :] = (bufs[acc, tile, here, :] + mid + h) * (1.0 / 3.0)
                return done

            lax.fori_loop(0, count, body, 0)

        prepare(u, first_row(1))

        def step(i, done):
            for which in range(STAGES):
                stage(which, i * STAGES + which + 1)
            return done

        lax.fori_loop(0, STEPS, step, 0)
        bottom = win - halo - size
        s = side_ref[0]
        for f in range(nfield):
            for tile in range(whole + (start > 0)):
                width = LANES if tile < whole else start
                cols = slice(tile * LANES, tile * LANES + width)
                for z in range(depth):
                    out_ref[f, z, :, cols] = bufs[u, tile, strided(z, bottom, f, size), :][:, :width]
                give_ref[f, :, cols] = bufs[u, tile, strided((s + 1) % depth, bottom, f, size), :][:, :width]
                mine_ref[f, :, cols] = bufs[u, tile, strided(s % depth, bottom, f, size), :][:, :width]
        if not final:
            for z in range(depth):
                for b in range(4):
                    for tile in range(tiles):
                        left_ref[b, tile, z] = bufs[b, tile, place(z, win - keep, keep), :]

    specs = [pl.BlockSpec(memory_space=pltpu.SMEM)]
    for array, at, edge, _ in blocks:
        if edge is None:
            specs.append(pl.BlockSpec(array.shape, lambda i: (0, 0, 0)))
        else:
            specs.append(pl.BlockSpec((nfield, depth, halo, xrows), (lambda i, at=at: (0, 0, at, 0))))
    specs.append(pl.BlockSpec((ycols, 2 * LANES), lambda i: (0, 0)))
    operands = [side, *(b[0] for b in blocks), next(b[2] for b in blocks if b[2] is not None)]
    aliases = {}
    if carry is not None:
        operands += [carry, filled]
        specs += [pl.BlockSpec(carry.shape, lambda i: (0, 0, 0, 0, 0)), pl.BlockSpec(memory_space=pl.ANY)]
        aliases = {len(operands) - 1: 0}
    operands += [coef, mix]
    specs += [pl.BlockSpec(coef.shape, lambda i: (0, 0, 0)), pl.BlockSpec(mix.shape, lambda i: (0, 0))]
    part = jax.ShapeDtypeStruct((nfield, size, xrows), jnp.float32)
    part_spec = pl.BlockSpec((nfield, size, xrows), lambda i: (0, 0, 0))
    shapes = [jax.ShapeDtypeStruct(fields_t.shape, jnp.float32), part, part]
    out_specs = [pl.BlockSpec((nfield, depth, size, xrows), lambda i: (0, 0, index, 0)), part_spec, part_spec]
    if not final:
        left = (4, tiles, depth, keep * nfield, LANES)
        shapes.append(jax.ShapeDtypeStruct(left, jnp.float32))
        out_specs.append(pl.BlockSpec(left, lambda i: (0, 0, 0, 0, 0)))
    work = sum(-(-(win - old - (0 if old else 2 * k)) // span) for k in range(1, stages + 1)) * rows * lanes
    return pl.pallas_call(
        kernel,
        grid=(1,),
        in_specs=specs,
        out_specs=out_specs,
        out_shape=shapes,
        scratch_shapes=[pltpu.VMEM((4, tiles, depth * win * nfield, LANES), jnp.float32),
                        pltpu.VMEM((2 * rows, lanes), jnp.bfloat16),
                        pltpu.VMEM((rows, lanes), jnp.float32)],
        input_output_aliases=aliases,
        compiler_params=pltpu.CompilerParams(vmem_limit_bytes=40 << 20),
        cost_estimate=pl.CostEstimate(flops=4 * rows * work, bytes_accessed=8 * nfield * depth * size * xrows,
                                      transcendentals=work),
        name="stencil_chunk",
    )(*operands)


def ring(sizes, offsets):
    pairs = []
    for i in range(sizes[0]):
        for j in range(sizes[1]):
            pairs.append((i * sizes[1] + j, (i + offsets[0]) % sizes[0] * sizes[1] + (j + offsets[1]) % sizes[1]))
    return pairs


def halos(fields_t, edges, halo):
    sizes = (lax.axis_size("sim"), lax.axis_size(("grp", "gz")))
    nfield, depth, ycols, xrows = fields_t.shape

    def send(part, over_x, over_y):
        return lax.ppermute(part, AXES, ring(sizes, (over_x, over_y)))

    if sizes[0] == 2:
        edges = send(edges, 1, 0)
    else:
        edges = jnp.concatenate([send(edges[:, :LANES], -1, 0), send(edges[:, LANES:], 1, 0)], 1)
    joined = -(-2 * LANES // xrows)

    def rows(first, over_y):
        corner = edges[first:first + halo]
        corner = jnp.pad(corner, ((0, 0), (0, joined * xrows - 2 * LANES)))
        corner = jnp.transpose(corner.reshape(halo, joined, xrows), (1, 0, 2))
        part = fields_t[:, :, first:first + halo].reshape(nfield * depth, halo, xrows)
        return send(jnp.concatenate([part, corner], 0), 0, over_y)

    return edges, rows(ycols - halo, 1), rows(0, -1)


def gram_messages(gathered, basis_y, place):
    n_core, n_grp = len(gathered), len(gathered[0])
    n_pair, nf, ycols, rank = gathered[0][0].shape
    count = n_core * n_grp * n_pair * ycols
    half = count // 2
    ncols = basis_y.shape[1] // (n_grp * n_pair * n_core)
    wide = nf * rank

    def kernel(place_ref, by_ref, *refs):
        q_refs, refs = refs[:n_core * n_grp], refs[n_core * n_grp:]
        outs, (hi, lo, res) = refs[:2 * n_pair], refs[2 * n_pair:]
        s, z, x, c = (place_ref[i] for i in range(4))
        for dz in range(n_grp):
            for xx in range(n_pair):
                for dc in range(n_core):
                    row = pl.multiple_of((((z ^ dz) * n_pair + xx) * n_core + (c ^ dc)) * ycols, ycols)
                    for f in range(nf):
                        q = q_refs[dc * n_grp + dz][xx, f]
                        big = q.astype(jnp.bfloat16)
                        hi[pl.ds(row, ycols), f * rank:(f + 1) * rank] = big
                        lo[pl.ds(row, ycols), f * rank:(f + 1) * rank] = (q - big.astype(jnp.float32)).astype(jnp.bfloat16)
        dims = (((1,), (1,)), ((), ()))
        starts = [pl.multiple_of(((z * n_pair + (x ^ dx)) * n_core + c) * ycols, ycols) for dx in range(n_pair)]
        mine = jnp.concatenate([part[pl.ds(row, ycols), :] for part in (hi, lo) for row in starts], 0)
        n_rows = n_pair * ycols
        for ds in range(2):
            cols = pl.ds(pl.multiple_of((s ^ ds) * half, half), half)
            part = lax.dot_general(mine, hi[cols, :], dims, preferred_element_type=jnp.float32)
            part = part[:n_rows] + part[n_rows:]
            part += lax.dot_general(mine[:n_rows], lo[cols, :], dims, preferred_element_type=jnp.float32)
            for dx in range(n_pair):
                outs[2 * dx + ds][0:ycols, :] = part[dx * ycols:(dx + 1) * ycols]
        turned = (((0,), (0,)), ((), ()))
        core = lax.dot_general(by_ref[...], hi[...], turned, preferred_element_type=jnp.float32)
        core += lax.dot_general(by_ref[...], lo[...], turned, preferred_element_type=jnp.float32)
        res[...] = core
        keep = rank // 2
        for dx in range(n_pair):
            mine = res[pl.ds(pl.multiple_of(((z * n_pair + (x ^ dx)) * n_core + c) * ncols, ncols), ncols), :]
            packs = []
            for side in range(2):
                parts = [mine[:, f * rank + side * keep:f * rank + (side + 1) * keep] for f in range(nf)]
                parts.append(jnp.zeros((ncols, half - nf * keep), jnp.float32))
                packs.append(jnp.concatenate(parts, 1))
            for ds in range(2):
                outs[2 * dx + ds][ycols:ycols + ncols, :] = jnp.where((s ^ ds) == 0, packs[0], packs[1])

    return pl.pallas_call(
        kernel,
        in_specs=[pl.BlockSpec(memory_space=pltpu.SMEM)] + [pl.BlockSpec(memory_space=pltpu.VMEM)] * (1 + n_core * n_grp),
        out_shape=[jax.ShapeDtypeStruct((ycols + ncols, half), jnp.float32)] * (2 * n_pair),
        scratch_shapes=[pltpu.VMEM((count, wide), jnp.bfloat16)] * 2 + [pltpu.VMEM((basis_y.shape[1], wide), jnp.float32)],
        compiler_params=pltpu.CompilerParams(vmem_limit_bytes=32 << 20),
        cost_estimate=pl.CostEstimate(flops=6 * 2 * ycols * count * wide, bytes_accessed=8 * count * wide, transcendentals=0),
        name="gram_messages",
    )(place, basis_y, *(part for side in gathered for part in side))


def finish_y(pieces, place, nf, ycols, scale):
    rows, half = pieces[0].shape
    ncols = rows - ycols

    def kernel(place_ref, a_ref, b_ref, c_ref, d_ref, gram_ref, core_ref):
        s, x = place_ref[0], place_ref[2]
        refs = (a_ref, b_ref, c_ref, d_ref)
        gram_ref[...] = ((a_ref[0:ycols, :] + b_ref[0:ycols, :]) + (c_ref[0:ycols, :] + d_ref[0:ycols, :])) * scale
        r = core_ref.shape[3]
        for dx in range(2):
            for ds in range(2):
                piece = refs[2 * dx + ds][ycols:rows, :]
                for f in range(nf):
                    core_ref[(x ^ dx) * nf + f, s ^ ds] = piece[:, f * r:(f + 1) * r]

    def call(r):
        return pl.pallas_call(
            kernel,
            in_specs=[pl.BlockSpec(memory_space=pltpu.SMEM)] + [pl.BlockSpec(memory_space=pltpu.VMEM)] * 4,
            out_shape=(jax.ShapeDtypeStruct((ycols, half), jnp.float32),
                       jax.ShapeDtypeStruct((2 * nf, 2, ncols, r), jnp.float32)),
            name="finish_y",
        )(place, *pieces)

    return call


def after(value, *first):
    return lax.optimization_barrier((value, *first))[0]


def pairwise(state_t, mine, theirs, basis_x, basis_y):
    n_grp, n_gz = lax.axis_size("grp"), lax.axis_size("gz")
    nfield, depth, ycols, xrows = state_t.shape
    rank = basis_x.shape[1]
    size = 2 * n_grp * n_gz
    core_bit, pair_bit, near_bit, far_bit, sim_bit = 1, n_gz // 2, n_gz, 2 * n_gz, n_grp * n_gz
    s, z, gz = lax.axis_index("sim"), lax.axis_index("grp"), lax.axis_index("gz")
    x, c = gz // 2, gz % 2
    place = jnp.stack([s, z, x, c]).astype(jnp.int32)

    def swap(part, bits):
        return lax.ppermute(part, AXES, [(i, i ^ bits) for i in range(size)])

    def pick(part, index, axis):
        return lax.dynamic_index_in_dim(part, index, axis, keepdims=False)

    own_rows = lax.dynamic_slice_in_dim(basis_x, s * xrows, xrows, 0).astype(jnp.float32)
    their_rows = lax.dynamic_slice_in_dim(basis_x, (1 - s) * xrows, xrows, 0).astype(jnp.float32)

    same = jnp.einsum("fzyw,fzyx->wx", state_t, state_t, precision=high).reshape(2, 2, 2, ycols, xrows)
    same_send = pick(same, 1 - c, 2)
    same_got = swap(same_send, core_bit)

    proj = jnp.einsum("fyx,xr->fyr", mine, own_rows, precision=high) + jnp.einsum(
        "fyx,xr->fyr", theirs, their_rows, precision=high)
    proj = proj.reshape(2, nfield // 2, ycols, rank)
    q_send = pick(proj, 1 - x, 0)
    q_got = swap(q_send, pair_bit)

    cross = jnp.einsum("fyw,fyx->wx", after(theirs, q_send), mine, precision=high)
    cross = jnp.stack([cross, cross.T]).reshape(2, 2, 2, 2, ycols, xrows)
    cross_send = pick(cross, 1 - c, 3)
    cross_got = swap(cross_send, core_bit)

    same = pick(same, c, 2) + same_got
    same_send = pick(same, 1 - x, 1)
    same_got = swap(same_send, pair_bit)

    own = pick(proj, x, 0)
    pair = jnp.where(x == 0, jnp.stack([own, q_got]), jnp.stack([q_got, own]))
    far = swap(pair, far_bit)
    near = swap(pair, near_bit)

    cross = pick(cross, c, 3) + cross_got
    cross_here, cross_there = pick(cross, x, 2), pick(cross, 1 - x, 2)
    got_pair = swap(cross_there[0], pair_bit)
    got_sim = swap(cross_here[1], sim_bit)
    got_diag = swap(cross_there[1], sim_bit | pair_bit)

    both = swap(far, near_bit)
    near_core = swap(near, core_bit)
    pair_core = swap(pair, core_bit)
    far_core = swap(far, core_bit)
    at_home = z // 2 == s
    zero = z % 2
    same = pick(same, x, 1) + same_got
    cross = (cross_here[0] + got_pair) + (got_sim + got_diag)
    kept, passed = jnp.where(at_home, same, cross), jnp.where(at_home, cross, same)
    own_block = pick(kept, zero, 0)
    to_near, to_far, to_both = pick(kept, 1 - zero, 0), pick(passed, zero, 0), pick(passed, 1 - zero, 0)
    x_far = swap(to_far, far_bit)
    x_both = swap(to_both, far_bit | near_bit)
    x_near = swap(to_near, near_bit)

    both_core = swap(both, core_bit)
    gathered = [[pair, near, far, both], [pair_core, near_core, far_core, both_core]]
    messages = gram_messages(gathered, basis_y, place)
    y_diag = swap(messages[3], sim_bit | pair_bit)
    y_pair = swap(messages[2], pair_bit)
    y_sim = swap(messages[1], sim_bit)

    gram_x = (own_block + x_near) + (x_far + x_both)
    gram_x = gram_x * (1.0 / (nfield * depth * ycols * n_grp * n_gz))
    pieces = [messages[0], y_sim, y_pair, y_diag]
    gram_y, core = finish_y(pieces, place, nfield // 2, ycols, 1.0 / (nfield * depth * rank))(rank // 2)
    return gram_x.T, gram_y, jnp.transpose(core, (0, 1, 3, 2))


def collective(state, basis_x, basis_y):
    nfield, depth, x_rows, ycols = state.shape
    rank = basis_y.shape[1]
    n_y = lax.axis_size(("grp", "gz"))
    basis_xf = basis_x.astype(jnp.float32)
    basis_yf = basis_y.astype(jnp.float32)
    gram_rows = jnp.einsum(
        "fzxy,fzwy->xw", state, lax.all_gather(state, "sim", axis=2, tiled=True), precision=highest
    )
    own_basis = lax.dynamic_slice_in_dim(basis_xf, lax.axis_index("sim") * x_rows, x_rows, 0)
    partial_proj = jnp.einsum("xr,fzxy->fzry", own_basis, state, precision=highest)
    projected = lax.psum_scatter(partial_proj, "sim", scatter_dimension=2, tiled=True)
    gram_x = lax.psum_scatter(gram_rows, ("grp", "gz"), scatter_dimension=1, tiled=True) / (
        nfield * depth * ycols * n_y
    )
    rank_grp = rank // n_y
    rank_cols_y = lax.dynamic_slice_in_dim(basis_yf, lax.axis_index(("grp", "gz")) * rank_grp, rank_grp, 1)
    incoming = lax.all_gather(projected, ("grp", "gz"), axis=3, tiled=True)
    block = jnp.einsum("fzry,fzrv->yv", projected, incoming, precision=highest)
    core_part = jnp.einsum("vs,fzrv->fzrs", rank_cols_y, incoming, precision=highest)
    gram_y = lax.psum_scatter(block, "sim", scatter_dimension=1, tiled=True) / (nfield * depth * rank)
    return gram_x, gram_y, core_part


def is_paired(n_sim, n_grp, n_gz):
    return n_sim == 2 and n_grp == n_gz == 4


def compute(fields, diffusivity, velocity, coupling, basis_x, basis_y):
    halo = STAGES * STEPS
    fields_t = jnp.transpose(fields, (0, 1, 3, 2))
    nfield, depth, ycols, _ = fields_t.shape
    sizes = tuple(lax.axis_size(a) for a in AXES)
    paired = is_paired(*sizes) and depth == 2
    side = jnp.reshape(lax.axis_index("sim"), (1,)).astype(jnp.int32)
    span = LANES // (depth * nfield)
    coef, mix = coefficients(diffusivity, velocity, coupling, depth, span)
    edges, above, below = halos(fields_t, x_edges(fields_t, halo), halo)
    blocks = [(above, None, None, None)]
    blocks += [(fields_t, i, edges, i * halo) for i in range(ycols // halo)]
    blocks += [(below, None, None, None)]
    count = BANDS
    size = ycols // count
    cuts = [0] + [2 + size * (j + 1) // halo for j in range(count)]
    carry = state_t = None
    mine, theirs = [], []
    for j in range(count):
        out = stencil_chunk(fields_t, blocks[cuts[j]:cuts[j + 1]], carry, state_t, coef, mix, side, halo, span, j,
                            size, j == count - 1)
        state_t, give, keep = out[:3]
        carry = out[3] if j < count - 1 else None
        if paired:
            theirs.append(lax.ppermute(give, "sim", [(0, 1), (1, 0)]))
            mine.append(keep)
    state = jnp.transpose(state_t, (0, 1, 3, 2))
    if paired:
        statistics = pairwise(state_t, jnp.concatenate(mine, 1), jnp.concatenate(theirs, 1), basis_x, basis_y)
    else:
        statistics = collective(state, basis_x, basis_y)
    return (state, *statistics)


def solution(mesh):
    in_specs = (P(None, None, "sim", ("grp", "gz")), P(), P(), P(), P(), P())
    out_specs = (
        P(None, None, "sim", ("grp", "gz")),
        P("sim", ("grp", "gz")),
        P(("grp", "gz"), "sim"),
        P(None, None, "sim", ("grp", "gz")),
    )
    step = jax.shard_map(compute, mesh=mesh, in_specs=in_specs, out_specs=out_specs, check_vma=False)
    if not is_paired(mesh.shape["sim"], mesh.shape["grp"], mesh.shape["gz"]):
        return step
    return step
```
